32 devices in a mesh: parts: 2 (over y), tm: 16 (over z, x, core).
Axes of the slice: x: 2, y: 2, z: 4, core: 2. Of those that a mesh axis runs over, the one named last changes fastest.
Arguments:
- frames: bfloat16 [2048, 2048], P('tm', 'parts'), parts along dimension 1, may hold values from -6 to 6
- levels: int32 [2048], P(('parts', 'tm')), parts along dimension 0, may hold values from 0 to 15
- initial_state: float32 [256], P('parts'), parts along dimension 0, may hold values from -6 to 6
- transitions: float32 [16, 128, 128], replicated, may hold values from -1 to 1
- gain: bfloat16 [128, 128], replicated, may hold values from -1 to 1
- pixel_mode: int32 [2048], replicated, may hold values from 0 to 127
- pixel_weight: bfloat16 [2048], replicated, may hold values from 0.099609375 to 0.5
Outputs:
- estimates: float32 [2048, 128], P(('parts', 'tm')), parts along dimension 0
The draws below stay inside these ranges and needn't reach their ends.
There are 2 independent parts, one for each index of `parts`. The reference program is written for one: setup_inputs(seed, part) draws one part's arguments, and reference() takes and returns one part's arrays. A program takes and returns all parts, laid end to end along the dimension named above; an argument that names none is the same for every part. Nothing has to cross between parts.
All inputs are finite; a program needn't handle non-finite values.
Results may differ from the reference program's by a relative error of at most 0.0026.
Values may be sent and summed in bfloat16 or wider, within the bound.
A program may use at most 128 MiB of HBM per device.

```python
import math
import jax
import jax.numpy as jnp
from jax import lax

MODAL_DIMENSION = 128
PIX = 2048
LEVELS = 16
FRAMES = 1024


def mode_traits(key):
    modes = MODAL_DIMENSION // 2
    perm = jax.random.permutation(jax.random.fold_in(key, 1), modes)
    slow_count = modes // 2
    lagging_mode_choice = perm < slow_count
    keep = jax.random.uniform(jax.random.fold_in(key, 2), (modes,), jnp.float32, 0.3, 0.8)
    slow_rate = jnp.exp(jnp.log(keep) / FRAMES)
    fast_rate = jax.random.uniform(jax.random.fold_in(key, 3), (modes,), jnp.float32, 0.95, 0.975)
    capture_frequency = jnp.where(lagging_mode_choice, slow_rate, fast_rate)
    base = jax.random.uniform(jax.random.fold_in(key, 4), (modes,), jnp.float32, 0.05, 1.5)
    return (lagging_mode_choice, capture_frequency, base)


def draw_levels(key, part):
    holds = FRAMES // 16
    values = jax.random.randint(jax.random.fold_in(key, 21), (holds,), 1, LEVELS)
    values = values.at[0].set(LEVELS - 1)
    plan = jnp.repeat(values, 16)
    spots = jax.random.randint(jax.random.fold_in(key, 22), (4,), 0, FRAMES)
    plan = plan.at[spots].set(0)
    return plan.astype(jnp.int32)


def draw_transitions(key, part):
    lagging_mode_choice, capture_frequency, base = mode_traits(key)
    tension = jax.random.uniform(jax.random.fold_in(key, 5), (LEVELS,), jnp.float32, 0.7, 1.3)
    image_count_per_group = jax.random.uniform(jax.random.fold_in(key, 6), (MODAL_DIMENSION // 2,), jnp.float32, 0.5, 0.8)
    omega = base[None, :] * jnp.sqrt(tension)[:, None]
    tier_indices = jnp.arange(LEVELS)
    neighborhood_extent = capture_frequency[None, :] * jnp.where((tier_indices[:, None] == 0) & lagging_mode_choice[None, :], image_count_per_group[None, :], 1.0)
    cosine = neighborhood_extent * jnp.cos(omega)
    sine = neighborhood_extent * jnp.sin(omega)
    rows = jnp.arange(MODAL_DIMENSION)
    row_mode = rows // 2
    row_part = rows % 2
    partner = rows + 1 - 2 * row_part
    same = row_mode[:, None] == row_mode[None, :]
    cos_rows = cosine[:, row_mode][:, :, None]
    sin_rows = sine[:, row_mode][:, :, None]
    block = jnp.where(row_part[:, None] == row_part[None, :], cos_rows, jnp.where(row_part[:, None] < row_part[None, :], sin_rows, -sin_rows))
    rotation = jnp.where(same[None, :, :], block, 0.0)
    diag_val = cosine[:, row_mode]
    off_val = jnp.where(row_part[None, :] == 0, sine[:, row_mode], -sine[:, row_mode])
    amp = jnp.sqrt(jnp.float32(0.2) / (jnp.float32(MODAL_DIMENSION) * jnp.float32(FRAMES)))
    noise = jax.random.uniform(jax.random.fold_in(key, 7), (LEVELS, MODAL_DIMENSION, MODAL_DIMENSION), jnp.float32, -1.0, 1.0)
    upper = rows[:, None] < rows[None, :]
    lower = rows[:, None] > rows[None, :]
    skew = amp * jnp.where(upper[None, :, :], noise, jnp.where(lower[None, :, :], -jnp.transpose(noise, (0, 2, 1)), 0.0))
    skew_partner = jnp.take(skew, partner, axis=1)
    table = rotation + diag_val[:, :, None] * skew + off_val[:, :, None] * skew_partner
    return table.astype(jnp.float32)


def draw_gain(key, part):
    lagging_mode_choice, capture_frequency, base = mode_traits(key)
    row_rate = capture_frequency[jnp.arange(MODAL_DIMENSION) // 2]
    scale = jnp.sqrt(1.0 - row_rate * row_rate)
    raw = jax.random.normal(jax.random.fold_in(key, 8), (MODAL_DIMENSION, MODAL_DIMENSION), jnp.float32)
    return (scale[:, None] * raw / jnp.sqrt(jnp.float32(MODAL_DIMENSION))).astype(jnp.bfloat16)


def with_ends(entries, key, least, high):
    longest = entries.shape.index(max(entries.shape))
    spots = []
    for shift in (0, 1):
        where = [jax.random.randint(jax.random.fold_in(key, axis), (), 0, length) for axis, length in enumerate(entries.shape)]
        where[longest] = (where[longest] + shift) % entries.shape[longest]
        spots.append(tuple(where))
    return entries.at[spots[0]].set(least).at[spots[1]].set(high)


def shard_levels(key, dims, pieces, smallest, high):
    def one(dim, parts):
        steps = jax.random.uniform(jax.random.fold_in(jax.random.fold_in(key, 6), dim), (parts,), jnp.float32, smallest / len(pieces), high / len(pieces))
        return jnp.repeat(jnp.exp(steps), dims[dim] // parts).reshape((-1,) + (1,) * (len(dims) - dim - 1))

    level = one(*pieces[0])
    for cut in pieces[1:]:
        level = level * one(*cut)
    return level


def normal_values(own_key, shape, scale, bound, pieces=(), kind=jnp.bfloat16):
    result = jax.random.normal(own_key, shape, jnp.float32) * scale
    if len(pieces) > 0:
        result = shard_levels(own_key, shape, pieces, -0.22, 0.18) * result
    return jnp.clip(result, min=-bound, max=bound).astype(kind)


def setup_inputs(seed: int = 0, part: int = 0) -> dict:
    arg_keys = jax.random.split(jax.random.key(seed), 8)
    own_keys = jax.random.split(jax.random.fold_in(arg_keys[7], part), 8)
    frames = normal_values(own_keys[0], (PIX, FRAMES), 1.0, 6.0, ((0, 16),))
    levels = draw_levels(jax.random.fold_in(jax.random.fold_in(arg_keys[7], part), 71), part)
    initial_state = normal_values(own_keys[2], (MODAL_DIMENSION,), 1.0, 6.0, (), jnp.float32)
    transitions = draw_transitions(jax.random.fold_in(arg_keys[7], 71), part)
    gain = draw_gain(jax.random.fold_in(arg_keys[7], 71), part)
    pixel_mode = with_ends(jax.random.randint(arg_keys[5], (PIX,), 0, MODAL_DIMENSION), jax.random.fold_in(arg_keys[5], 1), 0, MODAL_DIMENSION - 1).astype(jnp.int32)
    pixel_weight = jnp.clip(jnp.exp(jax.random.uniform(arg_keys[6], (PIX,), jnp.float32, math.log(0.099609375), math.log(0.5))), 0.099609375, 0.5).astype(jnp.bfloat16)
    return {"frames": frames, "levels": levels, "initial_state": initial_state, "transitions": transitions, "gain": gain, "pixel_mode": pixel_mode, "pixel_weight": pixel_weight}


def reference(frames, levels, initial_state, transitions, gain, pixel_mode, pixel_weight):
    channels = jnp.arange(MODAL_DIMENSION, dtype=jnp.int32)
    projector = jnp.where(pixel_mode[None, :] == channels[:, None], pixel_weight[None, :], jnp.zeros((), jnp.bfloat16))
    measured = lax.dot_general(frames, projector, (((0,), (1,)), ((), ())), preferred_element_type=jnp.float32).astype(jnp.bfloat16)
    drive = lax.dot_general(measured, gain, (((1,), (1,)), ((), ())), preferred_element_type=jnp.float32)

    def advance(carried, inputs):
        tension, push = inputs
        moved = jnp.dot(transitions[tension], carried, precision=lax.Precision.HIGHEST) + push
        return moved, moved

    _, estimates = lax.scan(advance, initial_state, (levels, drive))
    return estimates
```

```python
import functools

import jax
import jax.numpy as jnp
from jax import lax
from jax.experimental import pallas as pl
from jax.experimental.pallas import tpu as pltpu
from jax.sharding import PartitionSpec as P

MESH = pl.DeviceIdType.MESH
F32 = jnp.float32
BF16 = jnp.bfloat16
STEPS = 8
GROUP = 4
PARTS = 4


def halves(x):
    high = x.astype(BF16)
    return high, (x - high.astype(F32)).astype(BF16)


def left_pair(x):
    high, low = halves(x)
    return jnp.concatenate([high, low], axis=1)


def right_pair(y):
    pair = left_pair(y)
    return jnp.concatenate([pair, pair], axis=0)


def joined(pair):
    return pair[:, : pair.shape[1] // 2] + pair[:, pair.shape[1] // 2 :]


def product(x, y):
    return joined(jnp.dot(left_pair(x), right_pair(y), preferred_element_type=F32))


def diagonal(size):
    return lax.broadcasted_iota(jnp.int32, (size, size), 0) == lax.broadcasted_iota(
        jnp.int32, (size, size), 1
    )


def to_column(eye, row):
    return jnp.sum(jnp.where(eye, row, 0.0), axis=1, keepdims=True)


def to_row(eye, column):
    return jnp.sum(jnp.where(eye, column, 0.0), axis=0, keepdims=True)


def row_step(eye, matrix, row, push):
    return jnp.sum(matrix * row + jnp.where(eye, push, 0.0), axis=1, keepdims=True)


def column_step(flipped, column, push):
    return jnp.sum(flipped * column, axis=0, keepdims=True) + push


def fused_kernel(
    n, group,
    levels, frames_in, table_in, gain_in, modes_in, weights_in, start_in,
    out,
    raw, turned, regrouped, table, flipped, pairs, prefix, heads, ends, tails, total, maps, segments, whole, planes, carriers, near,
    gain, modes, weights, start, projector, local, chunk_ends, shift, shifts, carried, carries,
    load_sem, send_sem, recv_sem, msend_sem, mrecv_sem, wsend_sem, wrecv_sem, ssend_sem, srecv_sem, ready,
):
    me = lax.axis_index("tm")
    place = lax.rem(me, group)
    home = me - place
    block, blocks = me // group, n // group
    span = out.shape[0]
    states = gain.shape[0]
    pixels = raw.shape[0]
    count = span // STEPS
    wide = n * span // PARTS
    frame_loads = [
        pltpu.make_async_copy(
            frames_in.at[:, pl.ds(k * wide, wide)], raw.at[:, pl.ds(k * wide, wide)], load_sem.at[k]
        )
        for k in range(PARTS)
    ]
    loads = [
        pltpu.make_async_copy(source, target, load_sem.at[PARTS + i])
        for i, (source, target) in enumerate(
            [(table_in, table), (gain_in, gain), (modes_in, modes), (weights_in, weights), (start_in, start)]
        )
    ]
    for load in frame_loads + loads:
        load.start()

    barrier = pltpu.get_barrier_semaphore()

    @pl.loop(me + 1, n)
    def _(other):
        pl.semaphore_signal(barrier, inc=1, device_id={"tm": other}, device_id_type=MESH)

    @pl.when(me > 0)
    def _():
        pl.semaphore_wait(barrier, me)

    @pl.loop(0, me)
    def _(other):
        pl.semaphore_signal(ready.at[me], inc=1, device_id={"tm": other}, device_id_type=MESH)

    def piece(target):
        return pltpu.make_async_remote_copy(
            src_ref=turned.at[pl.ds(pl.multiple_of(target * span, span), span)],
            dst_ref=regrouped.at[me],
            send_sem=send_sem.at[target],
            recv_sem=recv_sem.at[me],
            device_id={"tm": target},
            device_id_type=MESH,
        )

    def arrival(source):
        return pltpu.make_async_remote_copy(
            src_ref=regrouped.at[source],
            dst_ref=regrouped.at[source],
            send_sem=send_sem.at[source],
            recv_sem=recv_sem.at[source],
            device_id={"tm": source},
            device_id_type=MESH,
        )

    for k in range(PARTS):
        frame_loads[k].wait()
        for at in range(k * wide, (k + 1) * wide, 128):
            turned[at : at + 128] = raw[:, at : at + 128].T

        @pl.loop(jnp.minimum(k * n // PARTS, me), jnp.minimum((k + 1) * n // PARTS, me))
        def _(target):
            piece(target).start()

    def meet(low, high):
        @pl.loop(low, high)
        def _(target):
            pl.semaphore_wait(ready.at[target], 1)
            piece(target).start()

    regrouped[me] = turned[pl.ds(pl.multiple_of(me * span, span), span)]

    loads[0].wait()
    for level in range(table.shape[0]):
        other = table[level].T
        flipped[level] = other
        pairs[level] = right_pair(other)

    def prefix_step(step):
        for chunk in range(count):
            t = chunk * STEPS + step
            prefix[t] = joined(
                jnp.dot(left_pair(prefix[t - 1]), pairs[levels[t]], preferred_element_type=F32)
            )

    for chunk in range(count):
        prefix[chunk * STEPS] = flipped[levels[chunk * STEPS]]
    for step in range(1, STEPS // 2):
        prefix_step(step)
    meet(me + 1, home + group)
    for step in range(STEPS // 2, STEPS):
        prefix_step(step)

    spans = [prefix[chunk * STEPS + STEPS - 1] for chunk in range(count)]
    firsts = list(spans)
    for chunk in range(count):
        ends[chunk] = spans[chunk].T if chunk % 2 else spans[chunk]
    width = 1
    while width < count:
        for chunk in range(count):
            if chunk & width:
                base = (chunk // width) * width - 1
                spans[chunk] = product(spans[base], spans[chunk])
        width *= 2
    total[...] = spans[count - 1]
    maps[place] = spans[count - 1]

    def shared(away):
        other = home + lax.rem(place + away, group)
        return pltpu.make_async_remote_copy(
            src_ref=total,
            dst_ref=maps.at[place],
            send_sem=msend_sem.at[away],
            recv_sem=mrecv_sem.at[away],
            device_id={"tm": other},
            device_id_type=MESH,
        )

    for away in range(1, group):
        shared(away).start()
    meet(home + group, n)

    tail = firsts[count - 1]
    for chunk in range(count - 2, -1, -1):
        tails[chunk] = tail.T
        if chunk:
            tail = product(firsts[chunk], tail)
    for chunk in range(count - 1):
        heads[chunk] = spans[chunk].T

    for load in loads[1:]:
        load.wait()
    eye = diagonal(states)
    channels = lax.broadcasted_iota(jnp.int32, (states, pixels), 0)
    for k in range(n):
        projector[k] = (
            jnp.where(modes[k : k + 1] == channels, weights[k : k + 1].astype(F32), 0.0).T.astype(BF16)
        )
    unit = jnp.where(eye, 1.0, 0.0)
    none = jnp.zeros((states, states), F32)

    for away in range(1, group):
        shared(away).wait()
    chains = {}
    for i in range(group):
        chains[i, i] = unit
        chains[i, i + 1] = maps[i]
    for length in range(2, group + 1):
        for i in range(group - length + 1):
            half = i + length // 2
            chains[i, i + length] = product(chains[i, half], chains[half, i + length])
    whole[...] = chains[0, group]

    def forward(hops):
        return pltpu.make_async_remote_copy(
            src_ref=whole,
            dst_ref=planes.at[block],
            send_sem=wsend_sem.at[hops],
            recv_sem=wrecv_sem.at[hops],
            device_id={"tm": me + hops * group},
            device_id_type=MESH,
        )

    for hops in range(1, blocks):

        @pl.when(jnp.logical_and(block > 0, block + hops < blocks))
        def _():
            forward(hops).start()

    for i in range(group):
        segments[0, i] = chains[0, i]
        segments[1, i] = chains[i + 1, group] if i + 1 < group else unit

    for p in range(1, group):

        @pl.when(place == p)
        def _():
            for q in range(p):
                near[q] = chains[q + 1, p].T

    @pl.loop(place, group)
    def _(q):
        near[q] = none
        shifts[q] = jnp.zeros((8, states), F32)

    @pl.loop(home, n)
    def _(source):
        carries[source] = jnp.zeros((8, states), F32)

    seed = jnp.where(me == 0, jnp.sum(total[...].T * start[...], axis=1, keepdims=True), 0.0)

    measured = jnp.zeros((span, states), F32)
    for k in range(n):

        @pl.when(me != k)
        def _():
            arrival(k).wait_recv()

        measured += jnp.dot(regrouped[k], projector[k], preferred_element_type=F32)
    local[...] = lax.dot_general(
        measured.astype(BF16), gain[...], (((1,), (1,)), ((), ())), preferred_element_type=F32
    )
    held = [to_column(eye, local[c * STEPS : c * STEPS + 1]) for c in range(count)]
    for step in range(1, STEPS):
        for c in range(count):
            t = c * STEPS + step
            push = local[t : t + 1]
            if step % 2:
                held[c] = column_step(flipped[levels[t]], held[c], push)
                local[t : t + 1] = held[c]
            else:
                held[c] = row_step(eye, table[levels[t]], held[c], push)
                local[t : t + 1] = to_row(eye, held[c])
    gathered = jnp.where(eye, local[span - 1 : span], 0.0)
    for c in range(count - 1):
        gathered += tails[c] * local[c * STEPS + STEPS - 1 : c * STEPS + STEPS]
    final = jnp.sum(gathered, axis=1, keepdims=True) + seed
    shift[...] = jnp.broadcast_to(to_row(eye, final), shift.shape)
    carried[...] = jnp.broadcast_to(
        jnp.sum(segments[1, place] * final, axis=0, keepdims=True), carried.shape
    )

    def offset(source, target, ref, slots, at):
        return pltpu.make_async_remote_copy(
            src_ref=ref,
            dst_ref=slots.at[at],
            send_sem=ssend_sem.at[target],
            recv_sem=srecv_sem.at[source],
            device_id={"tm": target},
            device_id_type=MESH,
        )

    @pl.loop(home + group, n)
    def _(target):
        offset(me, target, carried, carries, me).start()

    @pl.loop(me + 1, home + group)
    def _(target):
        offset(me, target, shift, shifts, place).start()

    row = local[STEPS - 1 : STEPS]
    chunk_ends[0:1] = row
    for c in range(1, count):
        push = local[c * STEPS + STEPS - 1 : c * STEPS + STEPS]
        if c % 2:
            row = row_step(eye, ends[c], row, push)
            chunk_ends[c : c + 1] = to_row(eye, row)
        else:
            row = column_step(ends[c], row, push)
            chunk_ends[c : c + 1] = row

    carriers[block] = segments[0, place]
    for hops in range(1, blocks):

        @pl.when(block > hops)
        def _():
            pltpu.make_async_remote_copy(
                src_ref=planes.at[block - hops],
                dst_ref=planes.at[block - hops],
                send_sem=wsend_sem.at[hops],
                recv_sem=wrecv_sem.at[hops],
                device_id={"tm": me - hops * group},
                device_id_type=MESH,
            ).wait_recv()
            carriers[block - hops] = product(planes[block - hops], carriers[block - hops + 1])

    for k in range(1, blocks):
        carriers[k] = jnp.where(k <= block, carriers[k].T, 0.0)

    @pl.loop(0, home)
    def _(source):
        offset(source, source, carried, carries, source).wait_recv()

    @pl.loop(home, me)
    def _(source):
        offset(source, source, shift, shifts, lax.rem(source, group)).wait_recv()

    gathered = jnp.where(jnp.logical_and(eye, me == 0), start[...], 0.0)
    for q in range(group - 1):
        gathered += near[q] * shifts[q, 0:1]
    for k in range(1, blocks):
        sent = carries[(k - 1) * group, 0:1]
        for q in range(1, group):
            sent += carries[(k - 1) * group + q, 0:1]
        gathered += carriers[k] * sent
    entry = jnp.sum(gathered, axis=1, keepdims=True)
    inside = to_row(eye, entry)

    for c in range(count):
        if c:
            column = row_step(eye, heads[c - 1], inside, chunk_ends[c - 1 : c])
        else:
            column = entry
        for step in range(STEPS):
            t = c * STEPS + step
            out[t : t + 1] = column_step(prefix[t], column, local[t : t + 1])

    @pl.loop(0, n)
    def _(target):
        @pl.when(target != me)
        def _():
            piece(target).wait_send()

    for hops in range(1, blocks):

        @pl.when(jnp.logical_and(block > 0, block + hops < blocks))
        def _():
            forward(hops).wait_send()

    @pl.loop(home + group, n)
    def _(target):
        offset(me, target, carried, carries, me).wait_send()

    @pl.loop(me + 1, home + group)
    def _(target):
        offset(me, target, shift, shifts, place).wait_send()


VMEM = pl.BlockSpec(memory_space=pltpu.VMEM)
SMEM = pl.BlockSpec(memory_space=pltpu.SMEM)
HBM = pl.BlockSpec(memory_space=pltpu.HBM)
LIMIT = 62 * 1024 * 1024


def shards(n, frames, levels, initial_state, transitions, gain, pixel_mode, pixel_weight):
    group = GROUP
    while n % group:
        group //= 2
    blocks = n // group
    span = levels.shape[0]
    depth, states = transitions.shape[0], transitions.shape[1]
    pixels = frames.shape[0]
    count = span // STEPS
    square = (states, states)
    dma = pltpu.SemaphoreType.DMA
    return pl.pallas_call(
        functools.partial(fused_kernel, n, group),
        out_shape=pltpu.VMEM((span, states), F32),
        in_specs=[SMEM] + [HBM] * 6,
        out_specs=VMEM,
        scratch_shapes=[
            pltpu.VMEM((pixels, n * span), BF16),
            pltpu.VMEM((n * span, pixels), BF16),
            pltpu.VMEM((n, span, pixels), BF16),
            pltpu.VMEM((depth, *square), F32),
            pltpu.VMEM((depth, *square), F32),
            pltpu.VMEM((depth, 2 * states, 2 * states), BF16),
            pltpu.VMEM((span, *square), F32),
            pltpu.VMEM((count, *square), F32),
            pltpu.VMEM((count, *square), F32),
            pltpu.VMEM((count, *square), F32),
            pltpu.VMEM(square, F32),
            pltpu.VMEM((group, *square), F32),
            pltpu.VMEM((2, group, *square), F32),
            pltpu.VMEM(square, F32),
            pltpu.VMEM((blocks, *square), F32),
            pltpu.VMEM((blocks, *square), F32),
            pltpu.VMEM((group, *square), F32),
            pltpu.VMEM(square, BF16),
            pltpu.VMEM((n, pixels), jnp.int32),
            pltpu.VMEM((n, pixels), BF16),
            pltpu.VMEM((1, states), F32),
            pltpu.VMEM((n, pixels, states), BF16),
            pltpu.VMEM((span, states), F32),
            pltpu.VMEM((count, states), F32),
            pltpu.VMEM((8, states), F32),
            pltpu.VMEM((group, 8, states), F32),
            pltpu.VMEM((8, states), F32),
            pltpu.VMEM((n, 8, states), F32),
            dma((PARTS + 5,)),
            dma((n,)),
            dma((n,)),
            dma((group,)),
            dma((group,)),
            dma((blocks,)),
            dma((blocks,)),
            dma((n,)),
            dma((n,)),
            pltpu.SemaphoreType.REGULAR((n,)),
        ],
        compiler_params=pltpu.CompilerParams(
            collective_id=0, has_side_effects=True, vmem_limit_bytes=LIMIT
        ),
        name="filter",
    )(
        levels,
        frames,
        transitions,
        gain,
        pixel_mode.reshape(n, pixels),
        pixel_weight.reshape(n, pixels),
        initial_state.reshape(1, states),
    )


def solution(mesh):
    in_specs = (P("tm", "parts"), P(("parts", "tm")), P("parts"), P(), P(), P(), P())
    out_specs = P(("parts", "tm"), None)
    return jax.shard_map(
        functools.partial(shards, mesh.shape["tm"]),
        mesh=mesh,
        in_specs=in_specs,
        out_specs=out_specs,
        check_vma=False,
    )
```

```python
import functools

import jax
import jax.numpy as jnp
from jax import lax
from jax.experimental import pallas as pl
from jax.experimental.pallas import tpu as pltpu
from jax.sharding import PartitionSpec as P

MESH = pl.DeviceIdType.MESH
F32 = jnp.float32
BF16 = jnp.bfloat16
STEPS = 8
EARLY = 4
GROUP = 4
TOP = 32000.0


def halves(x):
    high = x.astype(BF16)
    return high, (x - high.astype(F32)).astype(BF16)


def left_pair(x):
    high, low = halves(x)
    return jnp.concatenate([high, low], axis=1)


def right_pair(y):
    pair = left_pair(y)
    return jnp.concatenate([pair, pair], axis=0)


def joined(pair):
    return pair[:, : pair.shape[1] // 2] + pair[:, pair.shape[1] // 2 :]


def product(x, y):
    return joined(jnp.dot(left_pair(x), right_pair(y), preferred_element_type=F32))


def diagonal(size):
    return lax.broadcasted_iota(jnp.int32, (size, size), 0) == lax.broadcasted_iota(
        jnp.int32, (size, size), 1
    )


def to_column(eye, row):
    return jnp.sum(jnp.where(eye, row, 0.0), axis=1, keepdims=True)


def to_row(eye, column):
    return jnp.sum(jnp.where(eye, column, 0.0), axis=0, keepdims=True)


def row_step(eye, matrix, row, push):
    return jnp.sum(matrix * row + jnp.where(eye, push, 0.0), axis=1, keepdims=True)


def column_step(flipped, column, push):
    return jnp.sum(flipped * column, axis=0, keepdims=True) + push


def fused_kernel(
    n,
    levels, frames_in, table_in, gain_in, modes_in, weights_in, start_in,
    out,
    raw, turned, sums, coded, arrived, scale, scales, table, flipped, pairs, prefix, foreign, heads, ends, tails, maps, segments, whole, planes, carriers, near,
    gain, modes, weights, heavy, start, projector, local, chunk_ends, shift, shifts, carried, carries, twin_levels,
    load_sem, swap_send, swap_recv, send_sem, recv_sem, ksend_sem, krecv_sem, lsend_sem, lrecv_sem, msend_sem, mrecv_sem, wsend_sem, wrecv_sem, ssend_sem, srecv_sem, ready, passed,
):
    group = GROUP
    me = lax.axis_index("tm")
    core, chip, chips = lax.rem(me, 2), me // 2, n // 2
    place = lax.rem(me, group)
    home = me - place
    sibling = me + 1 - 2 * core
    twin_place = lax.rem(place + 2, group)
    twin = home + twin_place
    block, blocks = me // group, n // group
    span = out.shape[0]
    states = gain.shape[0]
    pixels = raw.shape[1]
    count = span // STEPS
    loads = [
        pltpu.make_async_copy(source, target, load_sem.at[i])
        for i, (source, target) in enumerate(
            [
                (frames_in, raw.at[0]), (modes_in, modes), (weights_in, weights),
                (table_in, table), (gain_in, gain), (start_in, start),
            ]
        )
    ]
    for load in loads:
        load.start()

    barrier = pltpu.get_barrier_semaphore()

    def ahead(which):
        return jnp.maximum(which + lax.rem(which, 2) - 3, 0)

    far = ahead(chip)

    @pl.when(core == 0)
    def _():
        pl.semaphore_signal(barrier, inc=1, device_id={"tm": sibling}, device_id_type=MESH)

    @pl.loop(chip + 1, chips)
    def _(other):
        to = 2 * other + jnp.where(chip < ahead(other), 1, 0)
        pl.semaphore_signal(barrier, inc=1, device_id={"tm": to}, device_id_type=MESH)

    @pl.when(core == 1)
    def _():
        pl.semaphore_wait(barrier, 1 + 2 * far)
        pl.semaphore_signal(passed, inc=1, device_id={"tm": sibling}, device_id_type=MESH)

    @pl.when(core == 0)
    def _():
        pl.semaphore_wait(passed, 1)

    swap = pltpu.make_async_remote_copy(
        src_ref=frames_in, dst_ref=raw.at[1], send_sem=swap_send, recv_sem=swap_recv,
        device_id={"tm": sibling}, device_id_type=MESH,
    )
    swap.start()
    tell = pltpu.make_async_remote_copy(
        src_ref=levels, dst_ref=twin_levels, send_sem=lsend_sem, recv_sem=lrecv_sem,
        device_id={"tm": twin}, device_id_type=MESH,
    )

    def announce(low, high):
        @pl.loop(low, high)
        def _(other):
            pl.semaphore_signal(ready.at[chip], inc=1, device_id={"tm": 2 * other + core}, device_id_type=MESH)

    announce(0, far)

    def code(to):
        return pltpu.make_async_remote_copy(
            src_ref=coded.at[to], dst_ref=arrived.at[chip], send_sem=send_sem.at[to], recv_sem=recv_sem.at[chip],
            device_id={"tm": 2 * to + core}, device_id_type=MESH,
        )

    def weight(to):
        return pltpu.make_async_remote_copy(
            src_ref=scale, dst_ref=scales.at[chip], send_sem=ksend_sem.at[to], recv_sem=krecv_sem.at[chip],
            device_id={"tm": 2 * to + core}, device_id_type=MESH,
        )

    def arrival(source, slots, sent, received):
        return pltpu.make_async_remote_copy(
            src_ref=slots.at[source], dst_ref=slots.at[source], send_sem=sent.at[source], recv_sem=received.at[source],
            device_id={"tm": 2 * source + core}, device_id_type=MESH,
        )

    eye = diagonal(states)
    channels = lax.broadcasted_iota(jnp.int32, (states, pixels), 0)
    for load in loads[:3]:
        load.wait()
    heavy[...] = weights[...].astype(F32)
    for half, owner in enumerate((me, sibling)):
        projector[half * pixels : (half + 1) * pixels] = (
            jnp.where(
                modes[pl.ds(owner, 1)] == channels, heavy[pl.ds(owner, 1)], 0.0
            ).T.astype(BF16)
        )
    for at in range(0, n * span, 128):
        turned[at : at + 128, 0:pixels] = raw[0, :, at : at + 128].T
    loads[3].wait()
    for level in range(table.shape[0]):
        other = table[level].T
        flipped[level] = other
        pairs[level] = right_pair(other)

    @pl.when(core == 0)
    def _():
        @pl.when(chip > 0)
        def _():
            pl.semaphore_wait(barrier, 2 * (chip - far))

        pl.semaphore_signal(passed, inc=1, device_id={"tm": sibling}, device_id_type=MESH)

    @pl.when(core == 1)
    def _():
        pl.semaphore_wait(passed, 1)

    announce(far, chip)

    @pl.when(place >= 2)
    def _():
        tell.start()

    swap.wait()
    for at in range(0, n * span, 128):
        turned[at : at + 128, pixels : 2 * pixels] = raw[1, :, at : at + 128].T

    most = jnp.zeros((1, states), F32)
    for k in range(chips):
        sums[k] = jnp.dot(
            turned[pl.ds(pl.multiple_of((2 * k + core) * span, span), span)],
            projector[...],
            preferred_element_type=F32,
        )
        most = jnp.maximum(most, jnp.max(jnp.abs(sums[k]), axis=0, keepdims=True))
    most = jnp.maximum(most, 1e-30)
    scale[...] = most * (1.0 / TOP)
    finer = TOP / most
    for k in range(chips):
        coded[k] = jnp.round(sums[k] * finer).astype(jnp.int32).astype(jnp.int16)

    @pl.loop(0, chip)
    def _(to):
        code(to).start()
        weight(to).start()

    arrived[chip] = coded[chip]
    scales[chip] = scale[...]

    def prefix_step(step):
        for chunk in range(count):
            t = chunk * STEPS + step
            prefix[t] = joined(
                jnp.dot(left_pair(prefix[t - 1]), pairs[levels[t]], preferred_element_type=F32)
            )

    for chunk in range(count):
        prefix[chunk * STEPS] = flipped[levels[chunk * STEPS]]
    for step in range(1, EARLY):
        prefix_step(step)

    def meet(low, high):
        @pl.loop(jnp.minimum(low, chips), jnp.minimum(high, chips))
        def _(other):
            pl.semaphore_wait(ready.at[other], 1)
            code(other).start()
            weight(other).start()

            @pl.when(other == twin // 2)
            def _():
                tell.start()

    meet(chip + 1, 2 * block + 2)
    for step in range(EARLY, STEPS):
        prefix_step(step)

    meet(2 * block + 2, 2 * block + 4)
    spans = [prefix[chunk * STEPS + STEPS - 1] for chunk in range(count)]
    firsts = list(spans)
    for chunk in range(count):
        ends[chunk] = spans[chunk].T if chunk % 2 else spans[chunk]
    width = 1
    while width < count:
        for chunk in range(count):
            if chunk & width:
                base = (chunk // width) * width - 1
                spans[chunk] = product(spans[base], spans[chunk])
        width *= 2
    maps[place] = spans[count - 1]

    def shared(which):
        at = (place, twin_place)[which]
        return pltpu.make_async_remote_copy(
            src_ref=maps.at[at], dst_ref=maps.at[at], send_sem=msend_sem.at[which], recv_sem=mrecv_sem.at[which],
            device_id={"tm": sibling}, device_id_type=MESH,
        )

    shared(0).start()

    meet(2 * block + 4, 2 * block + 6)
    tell.wait()
    for chunk in range(count):
        foreign[chunk] = flipped[twin_levels[chunk * STEPS]]
    for step in range(1, STEPS):
        for chunk in range(count):
            foreign[chunk] = joined(
                jnp.dot(
                    left_pair(foreign[chunk]), pairs[twin_levels[chunk * STEPS + step]],
                    preferred_element_type=F32,
                )
            )
    others = [foreign[chunk] for chunk in range(count)]
    while len(others) > 1:
        others = [product(others[i], others[i + 1]) for i in range(0, len(others), 2)]
    maps[twin_place] = others[0]
    shared(1).start()

    meet(2 * block + 6, chips)

    tail = firsts[count - 1]
    for chunk in range(count - 2, -1, -1):
        tails[chunk] = tail.T
        if chunk:
            tail = product(firsts[chunk], tail)
    for chunk in range(count - 1):
        heads[chunk] = spans[chunk].T

    for load in loads[4:]:
        load.wait()
    unit = jnp.where(eye, 1.0, 0.0)
    none = jnp.zeros((states, states), F32)

    def shared_in(which):
        at = lax.rem(sibling, group) if which == 0 else lax.rem(sibling + 2, group)
        return pltpu.make_async_remote_copy(
            src_ref=maps.at[at], dst_ref=maps.at[at], send_sem=msend_sem.at[which], recv_sem=mrecv_sem.at[which],
            device_id={"tm": sibling}, device_id_type=MESH,
        )

    for which in range(2):
        shared_in(which).wait_recv()
        shared(which).wait_send()
    chains = {}
    for i in range(group):
        chains[i, i] = unit
        chains[i, i + 1] = maps[i]
    for length in range(2, group + 1):
        for i in range(group - length + 1):
            half = i + length // 2
            chains[i, i + length] = product(chains[i, half], chains[half, i + length])
    whole[...] = chains[0, group]

    def forward(hops):
        return pltpu.make_async_remote_copy(
            src_ref=whole,
            dst_ref=planes.at[block],
            send_sem=wsend_sem.at[hops],
            recv_sem=wrecv_sem.at[hops],
            device_id={"tm": me + hops * group},
            device_id_type=MESH,
        )

    for hops in range(1, blocks):

        @pl.when(jnp.logical_and(block > 0, block + hops < blocks))
        def _():
            forward(hops).start()

    for i in range(group):
        segments[0, i] = chains[0, i]
        segments[1, i] = chains[i + 1, group] if i + 1 < group else unit

    for p in range(1, group):

        @pl.when(place == p)
        def _():
            for q in range(p):
                near[q] = chains[q + 1, p].T

    @pl.loop(place, group)
    def _(q):
        near[q] = none
        shifts[q] = jnp.zeros((8, states), F32)

    @pl.loop(home, n)
    def _(source):
        carries[source] = jnp.zeros((8, states), F32)

    seed = jnp.where(me == 0, jnp.sum(maps[0].T * start[...], axis=1, keepdims=True), 0.0)

    measured = jnp.zeros((span, states), F32)
    for k in range(chips):

        @pl.when(chip != k)
        def _():
            arrival(k, arrived, send_sem, recv_sem).wait_recv()
            arrival(k, scales, ksend_sem, krecv_sem).wait_recv()

        measured += arrived[k].astype(jnp.int32).astype(F32) * scales[k, 0:1]
    local[...] = lax.dot_general(
        measured.astype(BF16), gain[...], (((1,), (1,)), ((), ())), preferred_element_type=F32
    )
    held = [to_column(eye, local[c * STEPS : c * STEPS + 1]) for c in range(count)]
    for step in range(1, STEPS):
        for c in range(count):
            t = c * STEPS + step
            push = local[t : t + 1]
            if step % 2:
                held[c] = column_step(flipped[levels[t]], held[c], push)
                local[t : t + 1] = held[c]
            else:
                held[c] = row_step(eye, table[levels[t]], held[c], push)
                local[t : t + 1] = to_row(eye, held[c])
    gathered = jnp.where(eye, local[span - 1 : span], 0.0)
    for c in range(count - 1):
        gathered += tails[c] * local[c * STEPS + STEPS - 1 : c * STEPS + STEPS]
    final = jnp.sum(gathered, axis=1, keepdims=True) + seed
    shift[...] = jnp.broadcast_to(to_row(eye, final), shift.shape)
    carried[...] = jnp.broadcast_to(
        jnp.sum(segments[1, place] * final, axis=0, keepdims=True), carried.shape
    )

    def offset(source, target, ref, slots, at):
        return pltpu.make_async_remote_copy(
            src_ref=ref,
            dst_ref=slots.at[at],
            send_sem=ssend_sem.at[target],
            recv_sem=srecv_sem.at[source],
            device_id={"tm": target},
            device_id_type=MESH,
        )

    @pl.loop(home + group, n)
    def _(target):
        offset(me, target, carried, carries, me).start()

    @pl.loop(me + 1, home + group)
    def _(target):
        offset(me, target, shift, shifts, place).start()

    row = local[STEPS - 1 : STEPS]
    chunk_ends[0:1] = row
    for c in range(1, count):
        push = local[c * STEPS + STEPS - 1 : c * STEPS + STEPS]
        if c % 2:
            row = row_step(eye, ends[c], row, push)
            chunk_ends[c : c + 1] = to_row(eye, row)
        else:
            row = column_step(ends[c], row, push)
            chunk_ends[c : c + 1] = row

    carriers[block] = segments[0, place]
    for hops in range(1, blocks):

        @pl.when(block > hops)
        def _():
            pltpu.make_async_remote_copy(
                src_ref=planes.at[block - hops],
                dst_ref=planes.at[block - hops],
                send_sem=wsend_sem.at[hops],
                recv_sem=wrecv_sem.at[hops],
                device_id={"tm": me - hops * group},
                device_id_type=MESH,
            ).wait_recv()
            carriers[block - hops] = product(planes[block - hops], carriers[block - hops + 1])

    for k in range(1, blocks):
        carriers[k] = jnp.where(k <= block, carriers[k].T, 0.0)

    @pl.loop(0, home)
    def _(source):
        offset(source, source, carried, carries, source).wait_recv()

    @pl.loop(home, me)
    def _(source):
        offset(source, source, shift, shifts, lax.rem(source, group)).wait_recv()

    gathered = jnp.where(jnp.logical_and(eye, me == 0), start[...], 0.0)
    for q in range(group - 1):
        gathered += near[q] * shifts[q, 0:1]
    for k in range(1, blocks):
        sent = carries[(k - 1) * group, 0:1]
        for q in range(1, group):
            sent += carries[(k - 1) * group + q, 0:1]
        gathered += carriers[k] * sent
    entry = jnp.sum(gathered, axis=1, keepdims=True)
    inside = to_row(eye, entry)

    for c in range(count):
        if c:
            column = row_step(eye, heads[c - 1], inside, chunk_ends[c - 1 : c])
        else:
            column = entry
        for step in range(STEPS):
            t = c * STEPS + step
            out[t : t + 1] = column_step(prefix[t], column, local[t : t + 1])

    @pl.loop(0, chips)
    def _(to):
        @pl.when(to != chip)
        def _():
            code(to).wait_send()
            weight(to).wait_send()

    for hops in range(1, blocks):

        @pl.when(jnp.logical_and(block > 0, block + hops < blocks))
        def _():
            forward(hops).wait_send()

    @pl.loop(home + group, n)
    def _(target):
        offset(me, target, carried, carries, me).wait_send()

    @pl.loop(me + 1, home + group)
    def _(target):
        offset(me, target, shift, shifts, place).wait_send()


VMEM = pl.BlockSpec(memory_space=pltpu.VMEM)
SMEM = pl.BlockSpec(memory_space=pltpu.SMEM)
HBM = pl.BlockSpec(memory_space=pltpu.HBM)
LIMIT = 62 * 1024 * 1024


def shards(n, frames, levels, initial_state, transitions, gain, pixel_mode, pixel_weight):
    group, chips = GROUP, n // 2
    blocks = n // group
    span = levels.shape[0]
    depth, states = transitions.shape[0], transitions.shape[1]
    pixels = frames.shape[0]
    count = span // STEPS
    square = (states, states)
    dma = pltpu.SemaphoreType.DMA
    return pl.pallas_call(
        functools.partial(fused_kernel, n),
        out_shape=pltpu.VMEM((span, states), F32),
        in_specs=[SMEM] + [HBM] * 6,
        out_specs=VMEM,
        scratch_shapes=[
            pltpu.VMEM((2, pixels, n * span), BF16),
            pltpu.VMEM((n * span, 2 * pixels), BF16),
            pltpu.VMEM((chips, span, states), F32),
            pltpu.VMEM((chips, span, states), jnp.int16),
            pltpu.VMEM((chips, span, states), jnp.int16),
            pltpu.VMEM((1, states), F32),
            pltpu.VMEM((chips, 1, states), F32),
            pltpu.VMEM((depth, *square), F32),
            pltpu.VMEM((depth, *square), F32),
            pltpu.VMEM((depth, 2 * states, 2 * states), BF16),
            pltpu.VMEM((span, *square), F32),
            pltpu.VMEM((count, *square), F32),
            pltpu.VMEM((count, *square), F32),
            pltpu.VMEM((count, *square), F32),
            pltpu.VMEM((count, *square), F32),
            pltpu.VMEM((group, *square), F32),
            pltpu.VMEM((2, group, *square), F32),
            pltpu.VMEM(square, F32),
            pltpu.VMEM((blocks, *square), F32),
            pltpu.VMEM((blocks, *square), F32),
            pltpu.VMEM((group, *square), F32),
            pltpu.VMEM(square, BF16),
            pltpu.VMEM((n, pixels), jnp.int32),
            pltpu.VMEM((n, pixels), BF16),
            pltpu.VMEM((n, pixels), F32),
            pltpu.VMEM((1, states), F32),
            pltpu.VMEM((2 * pixels, states), BF16),
            pltpu.VMEM((span, states), F32),
            pltpu.VMEM((count, states), F32),
            pltpu.VMEM((8, states), F32),
            pltpu.VMEM((group, 8, states), F32),
            pltpu.VMEM((8, states), F32),
            pltpu.VMEM((n, 8, states), F32),
            pltpu.SMEM((span,), jnp.int32),
            dma((6,)),
            dma,
            dma,
            dma((chips,)),
            dma((chips,)),
            dma((chips,)),
            dma((chips,)),
            dma,
            dma,
            dma((2,)),
            dma((2,)),
            dma((blocks,)),
            dma((blocks,)),
            dma((n,)),
            dma((n,)),
            pltpu.SemaphoreType.REGULAR((chips,)),
            pltpu.SemaphoreType.REGULAR,
        ],
        compiler_params=pltpu.CompilerParams(
            collective_id=0, has_side_effects=True, vmem_limit_bytes=LIMIT
        ),
        name="filter",
    )(
        levels,
        frames,
        transitions,
        gain,
        pixel_mode.reshape(n, pixels),
        pixel_weight.reshape(n, pixels),
        initial_state.reshape(1, states),
    )


def solution(mesh):
    in_specs = (P("tm", "parts"), P(("parts", "tm")), P("parts"), P(), P(), P(), P())
    out_specs = P(("parts", "tm"), None)
    return jax.shard_map(
        functools.partial(shards, mesh.shape["tm"]),
        mesh=mesh,
        in_specs=in_specs,
        out_specs=out_specs,
        check_vma=False,
    )
```

```python
import functools

import jax
import jax.numpy as jnp
from jax import lax
from jax.experimental import pallas as pl
from jax.experimental.pallas import tpu as pltpu
from jax.sharding import PartitionSpec as P

MESH = pl.DeviceIdType.MESH
F32 = jnp.float32
BF16 = jnp.bfloat16
STEPS = 8
EARLY = 4
GROUP = 4
TOP = 32000.0


def halves(x):
    high = x.astype(BF16)
    return high, (x - high.astype(F32)).astype(BF16)


def left_pair(x):
    high, low = halves(x)
    return jnp.concatenate([high, low], axis=1)


def right_pair(y):
    pair = left_pair(y)
    return jnp.concatenate([pair, pair], axis=0)


def joined(pair):
    return pair[:, : pair.shape[1] // 2] + pair[:, pair.shape[1] // 2 :]


def product(x, y):
    return joined(jnp.dot(left_pair(x), right_pair(y), preferred_element_type=F32))


def diagonal(size):
    return lax.broadcasted_iota(jnp.int32, (size, size), 0) == lax.broadcasted_iota(
        jnp.int32, (size, size), 1
    )


def to_column(eye, row):
    return jnp.sum(jnp.where(eye, row, 0.0), axis=1, keepdims=True)


def to_row(eye, column):
    return jnp.sum(jnp.where(eye, column, 0.0), axis=0, keepdims=True)


def row_step(eye, matrix, row, push):
    return jnp.sum(matrix * row + jnp.where(eye, push, 0.0), axis=1, keepdims=True)


def column_step(flipped, column, push):
    return jnp.sum(flipped * column, axis=0, keepdims=True) + push


def fused_kernel(
    n,
    levels, frames_in, table_in, gain_in, modes_in, weights_in, start_in,
    out,
    raw, turned, sums, coded, arrived, scale, scales, table, flipped, pairs, prefix, foreign, heads, ends, tails, maps, segments, whole, planes, carriers, near,
    gain, modes, weights, heavy, start, projector, local, chunk_ends, shift, shifts, carried, carries, twin_levels,
    load_sem, swap_send, swap_recv, send_sem, recv_sem, ksend_sem, krecv_sem, lsend_sem, lrecv_sem, msend_sem, mrecv_sem, wsend_sem, wrecv_sem, rsend_sem, rrecv_sem, ssend_sem, srecv_sem, ready, passed,
):
    group = GROUP
    me = lax.axis_index("tm")
    core, chip, chips = lax.rem(me, 2), me // 2, n // 2
    place = lax.rem(me, group)
    home = me - place
    sibling = me + 1 - 2 * core
    twin_place = lax.rem(place + 2, group)
    twin = home + twin_place
    block, blocks = me // group, n // group
    span = out.shape[0]
    states = gain.shape[0]
    pixels = raw.shape[1]
    count = span // STEPS
    loads = [
        pltpu.make_async_copy(source, target, load_sem.at[i])
        for i, (source, target) in enumerate(
            [
                (frames_in, raw.at[0]), (modes_in, modes), (weights_in, weights),
                (table_in, table), (gain_in, gain), (start_in, start),
            ]
        )
    ]
    for load in loads:
        load.start()

    barrier = pltpu.get_barrier_semaphore()

    def ahead(which):
        return jnp.maximum(which + lax.rem(which, 2) - 3, 0)

    far = ahead(chip)

    @pl.when(core == 0)
    def _():
        pl.semaphore_signal(barrier, inc=1, device_id={"tm": sibling}, device_id_type=MESH)

    @pl.loop(chip + 1, chips)
    def _(other):
        to = 2 * other + jnp.where(chip < ahead(other), 1, 0)
        pl.semaphore_signal(barrier, inc=1, device_id={"tm": to}, device_id_type=MESH)

    @pl.when(place >= 2)
    def _():
        pl.semaphore_signal(barrier, inc=1, device_id={"tm": home}, device_id_type=MESH)

    @pl.when(core == 1)
    def _():
        pl.semaphore_wait(barrier, 1 + 2 * far)
        pl.semaphore_signal(passed, inc=1, device_id={"tm": sibling}, device_id_type=MESH)

    @pl.when(core == 0)
    def _():
        pl.semaphore_wait(passed, 1)

    swap = pltpu.make_async_remote_copy(
        src_ref=frames_in, dst_ref=raw.at[1], send_sem=swap_send, recv_sem=swap_recv,
        device_id={"tm": sibling}, device_id_type=MESH,
    )
    swap.start()
    tell = pltpu.make_async_remote_copy(
        src_ref=levels, dst_ref=twin_levels, send_sem=lsend_sem, recv_sem=lrecv_sem,
        device_id={"tm": twin}, device_id_type=MESH,
    )

    def announce(low, high):
        @pl.loop(low, high)
        def _(other):
            pl.semaphore_signal(ready.at[chip], inc=1, device_id={"tm": 2 * other + core}, device_id_type=MESH)

    announce(0, far)

    def code(to):
        return pltpu.make_async_remote_copy(
            src_ref=coded.at[to], dst_ref=arrived.at[chip], send_sem=send_sem.at[to], recv_sem=recv_sem.at[chip],
            device_id={"tm": 2 * to + core}, device_id_type=MESH,
        )

    def weight(to):
        return pltpu.make_async_remote_copy(
            src_ref=scale, dst_ref=scales.at[chip], send_sem=ksend_sem.at[to], recv_sem=krecv_sem.at[chip],
            device_id={"tm": 2 * to + core}, device_id_type=MESH,
        )

    def arrival(source, slots, sent, received):
        return pltpu.make_async_remote_copy(
            src_ref=slots.at[source], dst_ref=slots.at[source], send_sem=sent.at[source], recv_sem=received.at[source],
            device_id={"tm": 2 * source + core}, device_id_type=MESH,
        )

    eye = diagonal(states)
    channels = lax.broadcasted_iota(jnp.int32, (states, pixels), 0)
    for load in loads[:3]:
        load.wait()
    heavy[...] = weights[...].astype(F32)
    for half, owner in enumerate((me, sibling)):
        projector[half * pixels : (half + 1) * pixels] = (
            jnp.where(
                modes[pl.ds(owner, 1)] == channels, heavy[pl.ds(owner, 1)], 0.0
            ).T.astype(BF16)
        )
    for at in range(0, n * span, 128):
        turned[at : at + 128, 0:pixels] = raw[0, :, at : at + 128].T
    loads[3].wait()
    for level in range(table.shape[0]):
        other = table[level].T
        flipped[level] = other
        pairs[level] = right_pair(other)

    @pl.when(core == 0)
    def _():
        pl.semaphore_wait(barrier, 2 * (chip - far) + jnp.where(place < 2, 2, 0))
        pl.semaphore_signal(passed, inc=1, device_id={"tm": sibling}, device_id_type=MESH)

    @pl.when(core == 1)
    def _():
        pl.semaphore_wait(passed, 1)

    announce(far, chip)

    tell.start()
    swap.wait()
    for at in range(0, n * span, 128):
        turned[at : at + 128, pixels : 2 * pixels] = raw[1, :, at : at + 128].T

    most = jnp.zeros((1, states), F32)
    for k in range(chips):
        sums[k] = jnp.dot(
            turned[pl.ds(pl.multiple_of((2 * k + core) * span, span), span)],
            projector[...],
            preferred_element_type=F32,
        )
        most = jnp.maximum(most, jnp.max(jnp.abs(sums[k]), axis=0, keepdims=True))
    most = jnp.maximum(most, 1e-30)
    scale[...] = most * (1.0 / TOP)
    finer = TOP / most
    for k in range(chips):
        coded[k] = jnp.round(sums[k] * finer).astype(jnp.int32).astype(jnp.int16)

    @pl.loop(0, chip)
    def _(to):
        code(to).start()
        weight(to).start()

    arrived[chip] = coded[chip]
    scales[chip] = scale[...]

    def prefix_step(step):
        for chunk in range(count):
            t = chunk * STEPS + step
            prefix[t] = joined(
                jnp.dot(left_pair(prefix[t - 1]), pairs[levels[t]], preferred_element_type=F32)
            )

    for chunk in range(count):
        prefix[chunk * STEPS] = flipped[levels[chunk * STEPS]]
    for step in range(1, EARLY):
        prefix_step(step)

    def meet(low, high):
        @pl.loop(jnp.minimum(low, chips), jnp.minimum(high, chips))
        def _(other):
            pl.semaphore_wait(ready.at[other], 1)
            code(other).start()
            weight(other).start()

    meet(chip + 1, 2 * block + 4)
    for step in range(EARLY, STEPS):
        prefix_step(step)

    meet(2 * block + 4, chips)
    spans = [prefix[chunk * STEPS + STEPS - 1] for chunk in range(count)]
    firsts = list(spans)
    for chunk in range(count):
        ends[chunk] = spans[chunk].T if chunk % 2 else spans[chunk]
    width = 1
    while width < count:
        for chunk in range(count):
            if chunk & width:
                base = (chunk // width) * width - 1
                spans[chunk] = product(spans[base], spans[chunk])
        width *= 2
    maps[place] = spans[count - 1]

    def shared(which):
        at = (place, twin_place)[which]
        return pltpu.make_async_remote_copy(
            src_ref=maps.at[at], dst_ref=maps.at[at], send_sem=msend_sem.at[which], recv_sem=mrecv_sem.at[which],
            device_id={"tm": sibling}, device_id_type=MESH,
        )

    shared(0).start()

    tell.wait()
    for chunk in range(count):
        foreign[chunk] = flipped[twin_levels[chunk * STEPS]]
    for step in range(1, STEPS):
        for chunk in range(count):
            foreign[chunk] = joined(
                jnp.dot(
                    left_pair(foreign[chunk]), pairs[twin_levels[chunk * STEPS + step]],
                    preferred_element_type=F32,
                )
            )
    others = [foreign[chunk] for chunk in range(count)]
    while len(others) > 1:
        others = [product(others[i], others[i + 1]) for i in range(0, len(others), 2)]
    maps[twin_place] = others[0]
    shared(1).start()

    tail = firsts[count - 1]
    for chunk in range(count - 2, -1, -1):
        tails[chunk] = tail.T
        if chunk:
            tail = product(firsts[chunk], tail)
    for chunk in range(count - 1):
        heads[chunk] = spans[chunk].T

    for load in loads[4:]:
        load.wait()
    unit = jnp.where(eye, 1.0, 0.0)
    none = jnp.zeros((states, states), F32)

    def shared_in(which):
        at = lax.rem(sibling, group) if which == 0 else lax.rem(sibling + 2, group)
        return pltpu.make_async_remote_copy(
            src_ref=maps.at[at], dst_ref=maps.at[at], send_sem=msend_sem.at[which], recv_sem=mrecv_sem.at[which],
            device_id={"tm": sibling}, device_id_type=MESH,
        )

    for which in range(2):
        shared_in(which).wait_recv()
        shared(which).wait_send()
    chains = {}
    for i in range(group):
        chains[i, i] = unit
        chains[i, i + 1] = maps[i]
    chains[0, 2] = product(chains[0, 1], chains[1, 2])
    chains[2, 4] = product(chains[2, 3], chains[3, 4])
    chains[0, 4] = product(chains[0, 2], chains[2, 4])
    whole[...] = chains[0, group]

    def forward(hops):
        return pltpu.make_async_remote_copy(
            src_ref=whole,
            dst_ref=planes.at[block],
            send_sem=wsend_sem.at[hops],
            recv_sem=wrecv_sem.at[hops],
            device_id={"tm": me + hops * group},
            device_id_type=MESH,
        )

    for hops in range(1, blocks):

        @pl.when((core == 1) & (block > 0) & (block + hops < blocks))
        def _():
            forward(hops).start()

    chains[1, 3] = product(chains[1, 2], chains[2, 3])
    chains[0, 3] = product(chains[0, 2], chains[2, 3])
    chains[1, 4] = product(chains[1, 2], chains[2, 4])
    for i in range(group):
        segments[0, i] = chains[0, i]
        segments[1, i] = chains[i + 1, group] if i + 1 < group else unit

    for p in range(1, group):

        @pl.when(place == p)
        def _():
            for q in range(p):
                near[q] = chains[q + 1, p].T

    @pl.loop(place, group)
    def _(q):
        near[q] = none
        shifts[q] = jnp.zeros((8, states), F32)

    @pl.loop(home, n)
    def _(source):
        carries[source] = jnp.zeros((8, states), F32)

    seed = jnp.where(me == 0, jnp.sum(maps[0].T * start[...], axis=1, keepdims=True), 0.0)

    measured = jnp.zeros((span, states), F32)
    for k in range(chips):

        @pl.when(chip != k)
        def _():
            arrival(k, arrived, send_sem, recv_sem).wait_recv()
            arrival(k, scales, ksend_sem, krecv_sem).wait_recv()

        measured += arrived[k].astype(jnp.int32).astype(F32) * scales[k, 0:1]
    local[...] = lax.dot_general(
        measured.astype(BF16), gain[...], (((1,), (1,)), ((), ())), preferred_element_type=F32
    )
    held = [to_column(eye, local[c * STEPS : c * STEPS + 1]) for c in range(count)]
    for step in range(1, STEPS):
        for c in range(count):
            t = c * STEPS + step
            push = local[t : t + 1]
            if step % 2:
                held[c] = column_step(flipped[levels[t]], held[c], push)
                local[t : t + 1] = held[c]
            else:
                held[c] = row_step(eye, table[levels[t]], held[c], push)
                local[t : t + 1] = to_row(eye, held[c])
    gathered = jnp.where(eye, local[span - 1 : span], 0.0)
    for c in range(count - 1):
        gathered += tails[c] * local[c * STEPS + STEPS - 1 : c * STEPS + STEPS]
    final = jnp.sum(gathered, axis=1, keepdims=True) + seed
    shift[...] = jnp.broadcast_to(to_row(eye, final), shift.shape)
    carried[...] = jnp.broadcast_to(
        jnp.sum(segments[1, place] * final, axis=0, keepdims=True), carried.shape
    )

    def offset(source, target, ref, slots, at):
        return pltpu.make_async_remote_copy(
            src_ref=ref,
            dst_ref=slots.at[at],
            send_sem=ssend_sem.at[target],
            recv_sem=srecv_sem.at[source],
            device_id={"tm": target},
            device_id_type=MESH,
        )

    @pl.loop(home + group, n)
    def _(target):
        offset(me, target, carried, carries, me).start()

    @pl.loop(me + 1, home + group)
    def _(target):
        offset(me, target, shift, shifts, place).start()

    def relay(hops):
        return pltpu.make_async_remote_copy(
            src_ref=planes.at[block - hops], dst_ref=planes.at[block - hops],
            send_sem=rsend_sem.at[hops], recv_sem=rrecv_sem.at[hops],
            device_id={"tm": sibling}, device_id_type=MESH,
        )

    for hops in range(1, blocks):

        @pl.when((core == 1) & (block > hops))
        def _():
            pltpu.make_async_remote_copy(
                src_ref=planes.at[block - hops],
                dst_ref=planes.at[block - hops],
                send_sem=wsend_sem.at[hops],
                recv_sem=wrecv_sem.at[hops],
                device_id={"tm": me - hops * group},
                device_id_type=MESH,
            ).wait_recv()
            relay(hops).start()

    row = local[STEPS - 1 : STEPS]
    chunk_ends[0:1] = row
    for c in range(1, count):
        push = local[c * STEPS + STEPS - 1 : c * STEPS + STEPS]
        if c % 2:
            row = row_step(eye, ends[c], row, push)
            chunk_ends[c : c + 1] = to_row(eye, row)
        else:
            row = column_step(ends[c], row, push)
            chunk_ends[c : c + 1] = row

    carriers[block] = segments[0, place]
    for hops in range(1, blocks):

        @pl.when(block > hops)
        def _():
            @pl.when(core == 0)
            def _():
                relay(hops).wait_recv()

            carriers[block - hops] = product(planes[block - hops], carriers[block - hops + 1])

    for k in range(1, blocks):
        carriers[k] = jnp.where(k <= block, carriers[k].T, 0.0)

    @pl.loop(0, home)
    def _(source):
        offset(source, source, carried, carries, source).wait_recv()

    @pl.loop(home, me)
    def _(source):
        offset(source, source, shift, shifts, lax.rem(source, group)).wait_recv()

    gathered = jnp.where(jnp.logical_and(eye, me == 0), start[...], 0.0)
    for q in range(group - 1):
        gathered += near[q] * shifts[q, 0:1]
    for k in range(1, blocks):
        sent = carries[(k - 1) * group, 0:1]
        for q in range(1, group):
            sent += carries[(k - 1) * group + q, 0:1]
        gathered += carriers[k] * sent
    entry = jnp.sum(gathered, axis=1, keepdims=True)
    inside = to_row(eye, entry)

    for c in range(count):
        if c:
            column = row_step(eye, heads[c - 1], inside, chunk_ends[c - 1 : c])
        else:
            column = entry
        for step in range(STEPS):
            t = c * STEPS + step
            out[t : t + 1] = column_step(prefix[t], column, local[t : t + 1])

    @pl.loop(0, chips)
    def _(to):
        @pl.when(to != chip)
        def _():
            code(to).wait_send()
            weight(to).wait_send()

    for hops in range(1, blocks):

        @pl.when((core == 1) & (block > 0) & (block + hops < blocks))
        def _():
            forward(hops).wait_send()

        @pl.when((core == 1) & (block > hops))
        def _():
            relay(hops).wait_send()

    @pl.loop(home + group, n)
    def _(target):
        offset(me, target, carried, carries, me).wait_send()

    @pl.loop(me + 1, home + group)
    def _(target):
        offset(me, target, shift, shifts, place).wait_send()


VMEM = pl.BlockSpec(memory_space=pltpu.VMEM)
SMEM = pl.BlockSpec(memory_space=pltpu.SMEM)
HBM = pl.BlockSpec(memory_space=pltpu.HBM)
LIMIT = 62 * 1024 * 1024


def shards(n, frames, levels, initial_state, transitions, gain, pixel_mode, pixel_weight):
    group, chips = GROUP, n // 2
    blocks = n // group
    span = levels.shape[0]
    depth, states = transitions.shape[0], transitions.shape[1]
    pixels = frames.shape[0]
    count = span // STEPS
    square = (states, states)
    dma = pltpu.SemaphoreType.DMA
    return pl.pallas_call(
        functools.partial(fused_kernel, n),
        out_shape=pltpu.VMEM((span, states), F32),
        in_specs=[SMEM] + [HBM] * 6,
        out_specs=VMEM,
        scratch_shapes=[
            pltpu.VMEM((2, pixels, n * span), BF16),
            pltpu.VMEM((n * span, 2 * pixels), BF16),
            pltpu.VMEM((chips, span, states), F32),
            pltpu.VMEM((chips, span, states), jnp.int16),
            pltpu.VMEM((chips, span, states), jnp.int16),
            pltpu.VMEM((1, states), F32),
            pltpu.VMEM((chips, 1, states), F32),
            pltpu.VMEM((depth, *square), F32),
            pltpu.VMEM((depth, *square), F32),
            pltpu.VMEM((depth, 2 * states, 2 * states), BF16),
            pltpu.VMEM((span, *square), F32),
            pltpu.VMEM((count, *square), F32),
            pltpu.VMEM((count, *square), F32),
            pltpu.VMEM((count, *square), F32),
            pltpu.VMEM((count, *square), F32),
            pltpu.VMEM((group, *square), F32),
            pltpu.VMEM((2, group, *square), F32),
            pltpu.VMEM(square, F32),
            pltpu.VMEM((blocks, *square), F32),
            pltpu.VMEM((blocks, *square), F32),
            pltpu.VMEM((group, *square), F32),
            pltpu.VMEM(square, BF16),
            pltpu.VMEM((n, pixels), jnp.int32),
            pltpu.VMEM((n, pixels), BF16),
            pltpu.VMEM((n, pixels), F32),
            pltpu.VMEM((1, states), F32),
            pltpu.VMEM((2 * pixels, states), BF16),
            pltpu.VMEM((span, states), F32),
            pltpu.VMEM((count, states), F32),
            pltpu.VMEM((8, states), F32),
            pltpu.VMEM((group, 8, states), F32),
            pltpu.VMEM((8, states), F32),
            pltpu.VMEM((n, 8, states), F32),
            pltpu.SMEM((span,), jnp.int32),
            dma((6,)),
            dma,
            dma,
            dma((chips,)),
            dma((chips,)),
            dma((chips,)),
            dma((chips,)),
            dma,
            dma,
            dma((2,)),
            dma((2,)),
            dma((blocks,)),
            dma((blocks,)),
            dma((blocks,)),
            dma((blocks,)),
            dma((n,)),
            dma((n,)),
            pltpu.SemaphoreType.REGULAR((chips,)),
            pltpu.SemaphoreType.REGULAR,
        ],
        compiler_params=pltpu.CompilerParams(
            collective_id=0, has_side_effects=True, vmem_limit_bytes=LIMIT
        ),
        name="filter",
    )(
        levels,
        frames,
        transitions,
        gain,
        pixel_mode.reshape(n, pixels),
        pixel_weight.reshape(n, pixels),
        initial_state.reshape(1, states),
    )


def solution(mesh):
    in_specs = (P("tm", "parts"), P(("parts", "tm")), P("parts"), P(), P(), P(), P())
    out_specs = P(("parts", "tm"), None)
    return jax.shard_map(
        functools.partial(shards, mesh.shape["tm"]),
        mesh=mesh,
        in_specs=in_specs,
        out_specs=out_specs,
        check_vma=False,
    )
```

```python
import functools

import jax
import jax.numpy as jnp
from jax import lax
from jax.experimental import pallas as pl
from jax.experimental.pallas import tpu as pltpu
from jax.sharding import PartitionSpec as P

MESH = pl.DeviceIdType.MESH
F32 = jnp.float32
BF16 = jnp.bfloat16
STEPS = 8
EARLY = 4
GROUP = 4
TOP = 32000.0


def halves(x):
    high = x.astype(BF16)
    return high, (x - high.astype(F32)).astype(BF16)


def left_pair(x):
    high, low = halves(x)
    return jnp.concatenate([high, low], axis=1)


def right_pair(y):
    pair = left_pair(y)
    return jnp.concatenate([pair, pair], axis=0)


def joined(pair):
    return pair[:, : pair.shape[1] // 2] + pair[:, pair.shape[1] // 2 :]


def product(x, y):
    return joined(jnp.dot(left_pair(x), right_pair(y), preferred_element_type=F32))


def diagonal(size):
    return lax.broadcasted_iota(jnp.int32, (size, size), 0) == lax.broadcasted_iota(
        jnp.int32, (size, size), 1
    )


def to_column(eye, row):
    return jnp.sum(jnp.where(eye, row, 0.0), axis=1, keepdims=True)


def to_row(eye, column):
    return jnp.sum(jnp.where(eye, column, 0.0), axis=0, keepdims=True)


def row_step(eye, matrix, row, push):
    return jnp.sum(matrix * row + jnp.where(eye, push, 0.0), axis=1, keepdims=True)


def column_step(flipped, column, push):
    return jnp.sum(flipped * column, axis=0, keepdims=True) + push


def fused_kernel(
    n,
    levels, frames_in, table_in, gain_in, modes_in, weights_in, start_in,
    out,
    raw, turned, sums, coded, arrived, scale, scales, table, flipped, pairs, prefix, foreign, heads, ends, tails, maps, segments, whole, planes, carriers, near,
    gain, modes, weights, heavy, start, projector, local, chunk_ends, shift, shifts, carried, carries, twin_levels,
    load_sem, swap_send, swap_recv, send_sem, recv_sem, ksend_sem, krecv_sem, lsend_sem, lrecv_sem, msend_sem, mrecv_sem, wsend_sem, wrecv_sem, rsend_sem, rrecv_sem, ssend_sem, srecv_sem, crecv_sem, ready, passed,
):
    group = GROUP
    me = lax.axis_index("tm")
    core, chip, chips = lax.rem(me, 2), me // 2, n // 2
    place = lax.rem(me, group)
    home = me - place
    sibling = me + 1 - 2 * core
    twin_place = lax.rem(place + 2, group)
    twin = home + twin_place
    block, blocks = me // group, n // group
    span = out.shape[0]
    states = gain.shape[0]
    pixels = raw.shape[1]
    count = span // STEPS
    loads = [
        pltpu.make_async_copy(source, target, load_sem.at[i])
        for i, (source, target) in enumerate(
            [
                (frames_in, raw.at[0]), (modes_in, modes), (weights_in, weights),
                (table_in, table), (gain_in, gain), (start_in, start),
            ]
        )
    ]
    for load in loads:
        load.start()

    barrier = pltpu.get_barrier_semaphore()

    def ahead(which):
        return jnp.maximum(which + lax.rem(which, 2) - 3, 0)

    far = ahead(chip)

    @pl.when(core == 0)
    def _():
        pl.semaphore_signal(barrier, inc=1, device_id={"tm": sibling}, device_id_type=MESH)

    @pl.loop(chip + 1, chips)
    def _(other):
        to = 2 * other + jnp.where(chip < ahead(other), 1, 0)
        pl.semaphore_signal(barrier, inc=1, device_id={"tm": to}, device_id_type=MESH)

    @pl.when(place >= 2)
    def _():
        pl.semaphore_signal(barrier, inc=1, device_id={"tm": home}, device_id_type=MESH)

    @pl.when(core == 1)
    def _():
        pl.semaphore_wait(barrier, 1 + 2 * far)
        pl.semaphore_signal(passed, inc=1, device_id={"tm": sibling}, device_id_type=MESH)

    @pl.when(core == 0)
    def _():
        pl.semaphore_wait(passed, 1)

    swap = pltpu.make_async_remote_copy(
        src_ref=frames_in, dst_ref=raw.at[1], send_sem=swap_send, recv_sem=swap_recv,
        device_id={"tm": sibling}, device_id_type=MESH,
    )
    swap.start()
    tell = pltpu.make_async_remote_copy(
        src_ref=levels, dst_ref=twin_levels, send_sem=lsend_sem, recv_sem=lrecv_sem,
        device_id={"tm": twin}, device_id_type=MESH,
    )

    def announce(low, high):
        @pl.loop(low, high)
        def _(other):
            pl.semaphore_signal(ready.at[chip], inc=1, device_id={"tm": 2 * other + core}, device_id_type=MESH)

    announce(0, far)

    def code(to):
        return pltpu.make_async_remote_copy(
            src_ref=coded.at[to], dst_ref=arrived.at[chip], send_sem=send_sem.at[to], recv_sem=recv_sem.at[chip],
            device_id={"tm": 2 * to + core}, device_id_type=MESH,
        )

    def weight(to):
        return pltpu.make_async_remote_copy(
            src_ref=scale, dst_ref=scales.at[chip], send_sem=ksend_sem.at[to], recv_sem=krecv_sem.at[chip],
            device_id={"tm": 2 * to + core}, device_id_type=MESH,
        )

    def arrival(source, slots, sent, received):
        return pltpu.make_async_remote_copy(
            src_ref=slots.at[source], dst_ref=slots.at[source], send_sem=sent.at[source], recv_sem=received.at[source],
            device_id={"tm": 2 * source + core}, device_id_type=MESH,
        )

    eye = diagonal(states)
    channels = lax.broadcasted_iota(jnp.int32, (states, pixels), 0)
    for load in loads[:3]:
        load.wait()
    heavy[...] = weights[...].astype(F32)
    for half, owner in enumerate((me, sibling)):
        projector[half * pixels : (half + 1) * pixels] = (
            jnp.where(
                modes[pl.ds(owner, 1)] == channels, heavy[pl.ds(owner, 1)], 0.0
            ).T.astype(BF16)
        )
    for at in range(0, n * span, 128):
        turned[at : at + 128, 0:pixels] = raw[0, :, at : at + 128].T

    @pl.when(core == 0)
    def _():
        pl.semaphore_wait(barrier, 2 * (chip - far) + jnp.where(place < 2, 2, 0))
        pl.semaphore_signal(passed, inc=1, device_id={"tm": sibling}, device_id_type=MESH)

    @pl.when(core == 1)
    def _():
        pl.semaphore_wait(passed, 1)

    announce(far, chip)

    tell.start()
    swap.wait()
    for at in range(0, n * span, 128):
        turned[at : at + 128, pixels : 2 * pixels] = raw[1, :, at : at + 128].T

    most = jnp.zeros((1, states), F32)
    for k in range(chips):
        sums[k] = jnp.dot(
            turned[pl.ds(pl.multiple_of((2 * k + core) * span, span), span)],
            projector[...],
            preferred_element_type=F32,
        )
        most = jnp.maximum(most, jnp.max(jnp.abs(sums[k]), axis=0, keepdims=True))
    most = jnp.maximum(most, 1e-30)
    scale[...] = most * (1.0 / TOP)
    finer = TOP / most
    for k in range(chips):
        coded[k] = jnp.round(sums[k] * finer).astype(jnp.int32).astype(jnp.int16)

    @pl.loop(0, chip)
    def _(to):
        code(to).start()
        weight(to).start()

    arrived[chip] = coded[chip]
    scales[chip] = scale[...]

    loads[3].wait()
    for level in range(table.shape[0]):
        other = table[level].T
        flipped[level] = other
        pairs[level] = right_pair(other)

    def prefix_step(step):
        for chunk in range(count):
            t = chunk * STEPS + step
            prefix[t] = joined(
                jnp.dot(left_pair(prefix[t - 1]), pairs[levels[t]], preferred_element_type=F32)
            )

    for chunk in range(count):
        prefix[chunk * STEPS] = flipped[levels[chunk * STEPS]]
    for step in range(1, EARLY):
        prefix_step(step)

    def meet(low, high):
        @pl.loop(jnp.minimum(low, chips), jnp.minimum(high, chips))
        def _(other):
            pl.semaphore_wait(ready.at[other], 1)
            code(other).start()
            weight(other).start()

    meet(chip + 1, 2 * block + 4)
    for step in range(EARLY, STEPS):
        prefix_step(step)

    spans = [prefix[chunk * STEPS + STEPS - 1] for chunk in range(count)]
    firsts = list(spans)
    for chunk in range(count):
        ends[chunk] = spans[chunk].T if chunk % 2 else spans[chunk]
    width = 1
    while width < count:
        for chunk in range(count):
            if chunk & width:
                base = (chunk // width) * width - 1
                spans[chunk] = product(spans[base], spans[chunk])
        width *= 2
    maps[place] = spans[count - 1]

    def shared(which):
        at = (place, twin_place)[which]
        return pltpu.make_async_remote_copy(
            src_ref=maps.at[at], dst_ref=maps.at[at], send_sem=msend_sem.at[which], recv_sem=mrecv_sem.at[which],
            device_id={"tm": sibling}, device_id_type=MESH,
        )

    shared(0).start()

    meet(2 * block + 4, chips)
    tell.wait()
    for chunk in range(count):
        foreign[chunk] = flipped[twin_levels[chunk * STEPS]]
    for step in range(1, STEPS):
        for chunk in range(count):
            foreign[chunk] = joined(
                jnp.dot(
                    left_pair(foreign[chunk]), pairs[twin_levels[chunk * STEPS + step]],
                    preferred_element_type=F32,
                )
            )
    others = [foreign[chunk] for chunk in range(count)]
    while len(others) > 1:
        others = [product(others[i], others[i + 1]) for i in range(0, len(others), 2)]
    maps[twin_place] = others[0]
    shared(1).start()

    tail = firsts[count - 1]
    for chunk in range(count - 2, -1, -1):
        tails[chunk] = tail.T
        if chunk:
            tail = product(firsts[chunk], tail)
    for chunk in range(count - 1):
        heads[chunk] = spans[chunk].T

    for load in loads[4:]:
        load.wait()
    unit = jnp.where(eye, 1.0, 0.0)
    none = jnp.zeros((states, states), F32)

    def shared_in(which):
        at = lax.rem(sibling, group) if which == 0 else lax.rem(sibling + 2, group)
        return pltpu.make_async_remote_copy(
            src_ref=maps.at[at], dst_ref=maps.at[at], send_sem=msend_sem.at[which], recv_sem=mrecv_sem.at[which],
            device_id={"tm": sibling}, device_id_type=MESH,
        )

    for which in range(2):
        shared_in(which).wait_recv()
        shared(which).wait_send()
    chains = {}
    for i in range(group):
        chains[i, i] = unit
        chains[i, i + 1] = maps[i]
    chains[0, 2] = product(chains[0, 1], chains[1, 2])
    chains[2, 4] = product(chains[2, 3], chains[3, 4])
    chains[0, 4] = product(chains[0, 2], chains[2, 4])
    whole[...] = chains[0, group]

    def forward(hops):
        return pltpu.make_async_remote_copy(
            src_ref=whole,
            dst_ref=planes.at[block],
            send_sem=wsend_sem.at[hops],
            recv_sem=wrecv_sem.at[hops],
            device_id={"tm": me + hops * group},
            device_id_type=MESH,
        )

    for hops in range(1, blocks):

        @pl.when((core == 1) & (block > 0) & (block + hops < blocks))
        def _():
            forward(hops).start()

    chains[1, 3] = product(chains[1, 2], chains[2, 3])
    chains[0, 3] = product(chains[0, 2], chains[2, 3])
    chains[1, 4] = product(chains[1, 2], chains[2, 4])
    for i in range(group):
        segments[0, i] = chains[0, i]
        segments[1, i] = chains[i + 1, group] if i + 1 < group else unit

    for p in range(1, group):

        @pl.when(place == p)
        def _():
            for q in range(p):
                near[q] = chains[q + 1, p].T

    @pl.loop(place, group)
    def _(q):
        near[q] = none
        shifts[q] = jnp.zeros((8, states), F32)

    @pl.loop(home, n)
    def _(source):
        carries[source] = jnp.zeros((8, states), F32)

    seed = jnp.where(me == 0, jnp.sum(maps[0].T * start[...], axis=1, keepdims=True), 0.0)

    measured = jnp.zeros((span, states), F32)
    for k in range(chips):

        @pl.when(chip != k)
        def _():
            arrival(k, arrived, send_sem, recv_sem).wait_recv()
            arrival(k, scales, ksend_sem, krecv_sem).wait_recv()

        measured += arrived[k].astype(jnp.int32).astype(F32) * scales[k, 0:1]
    local[...] = lax.dot_general(
        measured.astype(BF16), gain[...], (((1,), (1,)), ((), ())), preferred_element_type=F32
    )
    held = [to_column(eye, local[c * STEPS : c * STEPS + 1]) for c in range(count)]
    for step in range(1, STEPS):
        for c in range(count):
            t = c * STEPS + step
            push = local[t : t + 1]
            if step % 2:
                held[c] = column_step(flipped[levels[t]], held[c], push)
                local[t : t + 1] = held[c]
            else:
                held[c] = row_step(eye, table[levels[t]], held[c], push)
                local[t : t + 1] = to_row(eye, held[c])
    gathered = jnp.where(eye, local[span - 1 : span], 0.0)
    for c in range(count - 1):
        gathered += tails[c] * local[c * STEPS + STEPS - 1 : c * STEPS + STEPS]
    final = jnp.sum(gathered, axis=1, keepdims=True) + seed
    shift[...] = jnp.broadcast_to(to_row(eye, final), shift.shape)
    carried[...] = jnp.broadcast_to(
        jnp.sum(segments[1, place] * final, axis=0, keepdims=True), carried.shape
    )

    def offset(target, ref, slots, at, received):
        return pltpu.make_async_remote_copy(
            src_ref=ref,
            dst_ref=slots.at[at],
            send_sem=ssend_sem.at[target],
            recv_sem=received,
            device_id={"tm": target},
            device_id_type=MESH,
        )

    @pl.loop(home + group, n)
    def _(target):
        offset(target, carried, carries, me, crecv_sem.at[block]).start()

    @pl.loop(me + 1, home + group)
    def _(target):
        offset(target, shift, shifts, place, srecv_sem.at[place]).start()

    def relay(hops):
        return pltpu.make_async_remote_copy(
            src_ref=planes.at[block - hops], dst_ref=planes.at[block - hops],
            send_sem=rsend_sem.at[hops], recv_sem=rrecv_sem.at[hops],
            device_id={"tm": sibling}, device_id_type=MESH,
        )

    for hops in range(1, blocks):

        @pl.when((core == 1) & (block > hops))
        def _():
            pltpu.make_async_remote_copy(
                src_ref=planes.at[block - hops],
                dst_ref=planes.at[block - hops],
                send_sem=wsend_sem.at[hops],
                recv_sem=wrecv_sem.at[hops],
                device_id={"tm": me - hops * group},
                device_id_type=MESH,
            ).wait_recv()
            relay(hops).start()

    row = local[STEPS - 1 : STEPS]
    chunk_ends[0:1] = row
    for c in range(1, count):
        push = local[c * STEPS + STEPS - 1 : c * STEPS + STEPS]
        if c % 2:
            row = row_step(eye, ends[c], row, push)
            chunk_ends[c : c + 1] = to_row(eye, row)
        else:
            row = column_step(ends[c], row, push)
            chunk_ends[c : c + 1] = row

    carriers[block] = segments[0, place]
    for hops in range(1, blocks):

        @pl.when(block > hops)
        def _():
            @pl.when(core == 0)
            def _():
                relay(hops).wait_recv()

            carriers[block - hops] = product(planes[block - hops], carriers[block - hops + 1])

    for k in range(1, blocks):
        carriers[k] = jnp.where(k <= block, carriers[k].T, 0.0)

    @pl.loop(0, chips)
    def _(to):
        @pl.when(to != chip)
        def _():
            code(to).wait_send()
            weight(to).wait_send()

    for hops in range(1, blocks):

        @pl.when((core == 1) & (block > 0) & (block + hops < blocks))
        def _():
            forward(hops).wait_send()

        @pl.when((core == 1) & (block > hops))
        def _():
            relay(hops).wait_send()

    @pl.loop(home + group, n)
    def _(target):
        offset(target, carried, carries, me, crecv_sem.at[block]).wait_send()

    @pl.loop(me + 1, home + group)
    def _(target):
        offset(target, shift, shifts, place, srecv_sem.at[place]).wait_send()

    for plane in range(blocks - 1):

        @pl.when(block > plane)
        def _():
            four = carries.at[pl.ds(plane * group, group)]
            pltpu.make_async_remote_copy(
                src_ref=four, dst_ref=four, send_sem=ssend_sem.at[plane], recv_sem=crecv_sem.at[plane],
                device_id={"tm": sibling}, device_id_type=MESH,
            ).wait_recv()

    @pl.loop(home, me)
    def _(source):
        at = lax.rem(source, group)
        offset(source, shift, shifts, at, srecv_sem.at[at]).wait_recv()

    gathered = jnp.where(jnp.logical_and(eye, me == 0), start[...], 0.0)
    for q in range(group - 1):
        gathered += near[q] * shifts[q, 0:1]
    for k in range(1, blocks):
        sent = carries[(k - 1) * group, 0:1]
        for q in range(1, group):
            sent += carries[(k - 1) * group + q, 0:1]
        gathered += carriers[k] * sent
    entry = jnp.sum(gathered, axis=1, keepdims=True)
    inside = to_row(eye, entry)

    for c in range(count):
        if c:
            column = row_step(eye, heads[c - 1], inside, chunk_ends[c - 1 : c])
        else:
            column = entry
        for step in range(STEPS):
            t = c * STEPS + step
            out[t : t + 1] = column_step(prefix[t], column, local[t : t + 1])


VMEM = pl.BlockSpec(memory_space=pltpu.VMEM)
SMEM = pl.BlockSpec(memory_space=pltpu.SMEM)
HBM = pl.BlockSpec(memory_space=pltpu.HBM)
LIMIT = 62 * 1024 * 1024


def shards(n, frames, levels, initial_state, transitions, gain, pixel_mode, pixel_weight):
    group, chips = GROUP, n // 2
    blocks = n // group
    span = levels.shape[0]
    depth, states = transitions.shape[0], transitions.shape[1]
    pixels = frames.shape[0]
    count = span // STEPS
    square = (states, states)
    dma = pltpu.SemaphoreType.DMA
    return pl.pallas_call(
        functools.partial(fused_kernel, n),
        out_shape=pltpu.VMEM((span, states), F32),
        in_specs=[SMEM] + [HBM] * 6,
        out_specs=VMEM,
        scratch_shapes=[
            pltpu.VMEM((2, pixels, n * span), BF16),
            pltpu.VMEM((n * span, 2 * pixels), BF16),
            pltpu.VMEM((chips, span, states), F32),
            pltpu.VMEM((chips, span, states), jnp.int16),
            pltpu.VMEM((chips, span, states), jnp.int16),
            pltpu.VMEM((1, states), F32),
            pltpu.VMEM((chips, 1, states), F32),
            pltpu.VMEM((depth, *square), F32),
            pltpu.VMEM((depth, *square), F32),
            pltpu.VMEM((depth, 2 * states, 2 * states), BF16),
            pltpu.VMEM((span, *square), F32),
            pltpu.VMEM((count, *square), F32),
            pltpu.VMEM((count, *square), F32),
            pltpu.VMEM((count, *square), F32),
            pltpu.VMEM((count, *square), F32),
            pltpu.VMEM((group, *square), F32),
            pltpu.VMEM((2, group, *square), F32),
            pltpu.VMEM(square, F32),
            pltpu.VMEM((blocks, *square), F32),
            pltpu.VMEM((blocks, *square), F32),
            pltpu.VMEM((group, *square), F32),
            pltpu.VMEM(square, BF16),
            pltpu.VMEM((n, pixels), jnp.int32),
            pltpu.VMEM((n, pixels), BF16),
            pltpu.VMEM((n, pixels), F32),
            pltpu.VMEM((1, states), F32),
            pltpu.VMEM((2 * pixels, states), BF16),
            pltpu.VMEM((span, states), F32),
            pltpu.VMEM((count, states), F32),
            pltpu.VMEM((8, states), F32),
            pltpu.VMEM((group, 8, states), F32),
            pltpu.VMEM((8, states), F32),
            pltpu.VMEM((n, 8, states), F32),
            pltpu.SMEM((span,), jnp.int32),
            dma((6,)),
            dma,
            dma,
            dma((chips,)),
            dma((chips,)),
            dma((chips,)),
            dma((chips,)),
            dma,
            dma,
            dma((2,)),
            dma((2,)),
            dma((blocks,)),
            dma((blocks,)),
            dma((blocks,)),
            dma((blocks,)),
            dma((n,)),
            dma((group,)),
            dma((blocks,)),
            pltpu.SemaphoreType.REGULAR((chips,)),
            pltpu.SemaphoreType.REGULAR,
        ],
        compiler_params=pltpu.CompilerParams(
            collective_id=0, has_side_effects=True, vmem_limit_bytes=LIMIT
        ),
        name="filter",
    )(
        levels,
        frames,
        transitions,
        gain,
        pixel_mode.reshape(n, pixels),
        pixel_weight.reshape(n, pixels),
        initial_state.reshape(1, states),
    )


def solution(mesh):
    in_specs = (P("tm", "parts"), P(("parts", "tm")), P("parts"), P(), P(), P(), P())
    out_specs = P(("parts", "tm"), None)
    return jax.shard_map(
        functools.partial(shards, mesh.shape["tm"]),
        mesh=mesh,
        in_specs=in_specs,
        out_specs=out_specs,
        check_vma=False,
    )
```

```python
import functools

import jax
import jax.numpy as jnp
from jax import lax
from jax.experimental import pallas as pl
from jax.experimental.pallas import tpu as pltpu
from jax.sharding import PartitionSpec as P

MESH = pl.DeviceIdType.MESH
F32 = jnp.float32
BF16 = jnp.bfloat16
STEPS = 8
EARLY = 4
GROUP = 4
TOP = 32000.0


def halves(x):
    high = x.astype(BF16)
    return high, (x - high.astype(F32)).astype(BF16)


def left_pair(x):
    high, low = halves(x)
    return jnp.concatenate([high, low], axis=1)


def right_pair(y):
    pair = left_pair(y)
    return jnp.concatenate([pair, pair], axis=0)


def joined(pair):
    return pair[:, : pair.shape[1] // 2] + pair[:, pair.shape[1] // 2 :]


def product(x, y):
    return joined(jnp.dot(left_pair(x), right_pair(y), preferred_element_type=F32))


def diagonal(size):
    return lax.broadcasted_iota(jnp.int32, (size, size), 0) == lax.broadcasted_iota(
        jnp.int32, (size, size), 1
    )


def to_column(eye, row):
    return jnp.sum(jnp.where(eye, row, 0.0), axis=1, keepdims=True)


def to_row(eye, column):
    return jnp.sum(jnp.where(eye, column, 0.0), axis=0, keepdims=True)


def row_step(eye, matrix, row, push):
    return jnp.sum(matrix * row + jnp.where(eye, push, 0.0), axis=1, keepdims=True)


def column_step(flipped, column, push):
    return jnp.sum(flipped * column, axis=0, keepdims=True) + push


def fused_kernel(
    n,
    levels, frames_in, table_in, gain_in, modes_in, weights_in, start_in,
    out,
    raw, turned, sums, coded, arrived, scale, scales, table, flipped, pairs, prefix, foreign, heads, ends, tails, maps, segments, whole, planes, carriers, near,
    gain, modes, weights, heavy, start, projector, local, chunk_ends, shift, shifts, carried, carries, twin_levels,
    load_sem, swap_send, swap_recv, send_sem, recv_sem, ksend_sem, krecv_sem, lsend_sem, lrecv_sem, msend_sem, mrecv_sem, wsend_sem, wrecv_sem, rsend_sem, rrecv_sem, ssend_sem, srecv_sem, crecv_sem, ready, passed,
):
    group = GROUP
    me = lax.axis_index("tm")
    core, chip, chips = lax.rem(me, 2), me // 2, n // 2
    place = lax.rem(me, group)
    home = me - place
    sibling = me + 1 - 2 * core
    twin_place = lax.rem(place + 2, group)
    twin = home + twin_place
    block, blocks = me // group, n // group
    span = out.shape[0]
    states = gain.shape[0]
    pixels = raw.shape[1]
    count = span // STEPS
    loads = [
        pltpu.make_async_copy(source, target, load_sem.at[i])
        for i, (source, target) in enumerate(
            [
                (frames_in, raw.at[0]), (modes_in, modes), (weights_in, weights),
                (table_in, table), (gain_in, gain), (start_in, start),
            ]
        )
    ]
    for load in loads:
        load.start()

    barrier = pltpu.get_barrier_semaphore()

    def ahead(which):
        return jnp.maximum(which + lax.rem(which, 2) - 3, 0)

    far = ahead(chip)

    @pl.when(core == 0)
    def _():
        pl.semaphore_signal(barrier, inc=1, device_id={"tm": sibling}, device_id_type=MESH)

    @pl.loop(chip + 1, chips)
    def _(other):
        to = 2 * other + jnp.where(chip < ahead(other), 1, 0)
        pl.semaphore_signal(barrier, inc=1, device_id={"tm": to}, device_id_type=MESH)

    @pl.when(place >= 2)
    def _():
        pl.semaphore_signal(barrier, inc=1, device_id={"tm": home}, device_id_type=MESH)

    @pl.when(core == 1)
    def _():
        pl.semaphore_wait(barrier, 1 + 2 * far)
        pl.semaphore_signal(passed, inc=1, device_id={"tm": sibling}, device_id_type=MESH)

    @pl.when(core == 0)
    def _():
        pl.semaphore_wait(passed, 1)

    swap = pltpu.make_async_remote_copy(
        src_ref=frames_in, dst_ref=raw.at[1], send_sem=swap_send, recv_sem=swap_recv,
        device_id={"tm": sibling}, device_id_type=MESH,
    )
    swap.start()
    tell = pltpu.make_async_remote_copy(
        src_ref=levels, dst_ref=twin_levels, send_sem=lsend_sem, recv_sem=lrecv_sem,
        device_id={"tm": twin}, device_id_type=MESH,
    )

    def announce(low, high):
        @pl.loop(low, high)
        def _(other):
            pl.semaphore_signal(ready.at[chip], inc=1, device_id={"tm": 2 * other + core}, device_id_type=MESH)

    announce(0, far)

    def code(to):
        return pltpu.make_async_remote_copy(
            src_ref=coded.at[to], dst_ref=arrived.at[chip], send_sem=send_sem.at[to], recv_sem=recv_sem.at[chip],
            device_id={"tm": 2 * to + core}, device_id_type=MESH,
        )

    def weight(to):
        return pltpu.make_async_remote_copy(
            src_ref=scale, dst_ref=scales.at[chip], send_sem=ksend_sem.at[to], recv_sem=krecv_sem.at[chip],
            device_id={"tm": 2 * to + core}, device_id_type=MESH,
        )

    def arrival(source, slots, sent, received):
        return pltpu.make_async_remote_copy(
            src_ref=slots.at[source], dst_ref=slots.at[source], send_sem=sent.at[source], recv_sem=received.at[source],
            device_id={"tm": 2 * source + core}, device_id_type=MESH,
        )

    eye = diagonal(states)
    channels = lax.broadcasted_iota(jnp.int32, (states, pixels), 0)
    for load in loads[:3]:
        load.wait()
    heavy[...] = weights[...].astype(F32)
    for half, owner in enumerate((me, sibling)):
        projector[half * pixels : (half + 1) * pixels] = (
            jnp.where(
                modes[pl.ds(owner, 1)] == channels, heavy[pl.ds(owner, 1)], 0.0
            ).T.astype(BF16)
        )
    for at in range(0, n * span, 128):
        turned[at : at + 128, 0:pixels] = raw[0, :, at : at + 128].T

    @pl.when(core == 0)
    def _():
        pl.semaphore_wait(barrier, 2 * (chip - far) + jnp.where(place < 2, 2, 0))
        pl.semaphore_signal(passed, inc=1, device_id={"tm": sibling}, device_id_type=MESH)

    @pl.when(core == 1)
    def _():
        pl.semaphore_wait(passed, 1)

    announce(far, chip)

    tell.start()
    swap.wait()
    for at in range(0, n * span, 128):
        turned[at : at + 128, pixels : 2 * pixels] = raw[1, :, at : at + 128].T

    most = jnp.zeros((1, states), F32)
    for k in range(chips):
        sums[k] = jnp.dot(
            turned[pl.ds(pl.multiple_of((2 * k + core) * span, span), span)],
            projector[...],
            preferred_element_type=F32,
        )
        most = jnp.maximum(most, jnp.max(jnp.abs(sums[k]), axis=0, keepdims=True))
    most = jnp.maximum(most, 1e-30)
    scale[...] = most * (1.0 / TOP)
    finer = TOP / most
    for k in range(chips):
        coded[k] = jnp.round(sums[k] * finer).astype(jnp.int32).astype(jnp.int16)

    @pl.loop(0, chip)
    def _(to):
        weight(to).start()
        code(to).start()

    arrived[chip] = coded[chip]
    scales[chip] = scale[...]

    loads[3].wait()
    for level in range(table.shape[0]):
        other = table[level].T
        flipped[level] = other
        pairs[level] = right_pair(other)

    def prefix_step(step):
        for chunk in range(count):
            t = chunk * STEPS + step
            prefix[t] = joined(
                jnp.dot(left_pair(prefix[t - 1]), pairs[levels[t]], preferred_element_type=F32)
            )

    for chunk in range(count):
        prefix[chunk * STEPS] = flipped[levels[chunk * STEPS]]
    for step in range(1, EARLY):
        prefix_step(step)

    def meet(low, high):
        @pl.loop(jnp.minimum(low, chips), jnp.minimum(high, chips))
        def _(other):
            pl.semaphore_wait(ready.at[other], 1)
            weight(other).start()
            code(other).start()

    meet(chip + 1, 2 * block + 4)
    for step in range(EARLY, STEPS):
        prefix_step(step)

    spans = [prefix[chunk * STEPS + STEPS - 1] for chunk in range(count)]
    firsts = list(spans)
    for chunk in range(count):
        ends[chunk] = spans[chunk].T if chunk % 2 else spans[chunk]
    width = 1
    while width < count:
        for chunk in range(count):
            if chunk & width:
                base = (chunk // width) * width - 1
                spans[chunk] = product(spans[base], spans[chunk])
        width *= 2
    maps[place] = spans[count - 1]

    def shared(which):
        at = (place, twin_place)[which]
        return pltpu.make_async_remote_copy(
            src_ref=maps.at[at], dst_ref=maps.at[at], send_sem=msend_sem.at[which], recv_sem=mrecv_sem.at[which],
            device_id={"tm": sibling}, device_id_type=MESH,
        )

    shared(0).start()

    meet(2 * block + 4, chips)
    tell.wait()
    for chunk in range(count):
        foreign[chunk] = flipped[twin_levels[chunk * STEPS]]
    for step in range(1, STEPS):
        for chunk in range(count):
            foreign[chunk] = joined(
                jnp.dot(
                    left_pair(foreign[chunk]), pairs[twin_levels[chunk * STEPS + step]],
                    preferred_element_type=F32,
                )
            )
    others = [foreign[chunk] for chunk in range(count)]
    while len(others) > 1:
        others = [product(others[i], others[i + 1]) for i in range(0, len(others), 2)]
    maps[twin_place] = others[0]
    shared(1).start()

    tail = firsts[count - 1]
    for chunk in range(count - 2, -1, -1):
        tails[chunk] = tail.T
        if chunk:
            tail = product(firsts[chunk], tail)
    for chunk in range(count - 1):
        heads[chunk] = spans[chunk].T

    for load in loads[4:]:
        load.wait()
    turned_gain = gain[...].astype(F32).T.astype(BF16)
    unit = jnp.where(eye, 1.0, 0.0)
    none = jnp.zeros((states, states), F32)

    def shared_in(which):
        at = lax.rem(sibling, group) if which == 0 else lax.rem(sibling + 2, group)
        return pltpu.make_async_remote_copy(
            src_ref=maps.at[at], dst_ref=maps.at[at], send_sem=msend_sem.at[which], recv_sem=mrecv_sem.at[which],
            device_id={"tm": sibling}, device_id_type=MESH,
        )

    for which in range(2):
        shared_in(which).wait_recv()
        shared(which).wait_send()
    chains = {}
    for i in range(group):
        chains[i, i] = unit
        chains[i, i + 1] = maps[i]
    chains[0, 2] = product(chains[0, 1], chains[1, 2])
    chains[2, 4] = product(chains[2, 3], chains[3, 4])
    chains[0, 4] = product(chains[0, 2], chains[2, 4])
    whole[...] = chains[0, group]

    def forward(hops):
        return pltpu.make_async_remote_copy(
            src_ref=whole,
            dst_ref=planes.at[block],
            send_sem=wsend_sem.at[hops],
            recv_sem=wrecv_sem.at[hops],
            device_id={"tm": me + hops * group},
            device_id_type=MESH,
        )

    for hops in range(1, blocks):

        @pl.when((core == 1) & (block > 0) & (block + hops < blocks))
        def _():
            forward(hops).start()

    chains[1, 3] = product(chains[1, 2], chains[2, 3])
    chains[0, 3] = product(chains[0, 2], chains[2, 3])
    chains[1, 4] = product(chains[1, 2], chains[2, 4])
    for i in range(group):
        segments[0, i] = chains[0, i]
        segments[1, i] = chains[i + 1, group] if i + 1 < group else unit

    for p in range(1, group):

        @pl.when(place == p)
        def _():
            for q in range(p):
                near[q] = chains[q + 1, p].T

    @pl.loop(place, group)
    def _(q):
        near[q] = none
        shifts[q] = jnp.zeros((8, states), F32)

    @pl.loop(home, n)
    def _(source):
        carries[source] = jnp.zeros((8, states), F32)

    seed = jnp.where(me == 0, jnp.sum(maps[0].T * start[...], axis=1, keepdims=True), 0.0)

    measured = jnp.zeros((span, states), F32)
    for k in range(chips):

        @pl.when(chip != k)
        def _():
            arrival(k, arrived, send_sem, recv_sem).wait_recv()
            arrival(k, scales, ksend_sem, krecv_sem).wait_recv()

        measured += arrived[k].astype(jnp.int32).astype(F32) * scales[k, 0:1]
    local[...] = jnp.dot(measured.astype(BF16), turned_gain, preferred_element_type=F32)
    held = [to_column(eye, local[c * STEPS : c * STEPS + 1]) for c in range(count)]
    for step in range(1, STEPS):
        for c in range(count):
            t = c * STEPS + step
            push = local[t : t + 1]
            if step % 2:
                held[c] = column_step(flipped[levels[t]], held[c], push)
                local[t : t + 1] = held[c]
            else:
                held[c] = row_step(eye, table[levels[t]], held[c], push)
                local[t : t + 1] = to_row(eye, held[c])
    gathered = jnp.where(eye, local[span - 1 : span], 0.0)
    for c in range(count - 1):
        gathered += tails[c] * local[c * STEPS + STEPS - 1 : c * STEPS + STEPS]
    final = jnp.sum(gathered, axis=1, keepdims=True) + seed
    shift[...] = jnp.broadcast_to(to_row(eye, final), shift.shape)
    def offset(target, ref, slots, at, received):
        return pltpu.make_async_remote_copy(
            src_ref=ref,
            dst_ref=slots.at[at],
            send_sem=ssend_sem.at[target],
            recv_sem=received,
            device_id={"tm": target},
            device_id_type=MESH,
        )

    @pl.loop(me + 1, home + group)
    def _(target):
        offset(target, shift, shifts, place, srecv_sem.at[place]).start()

    carried[...] = jnp.broadcast_to(
        jnp.sum(segments[1, place] * final, axis=0, keepdims=True), carried.shape
    )

    @pl.loop(home + group, n)
    def _(target):
        offset(target, carried, carries, me, crecv_sem.at[block]).start()

    def relay(hops):
        return pltpu.make_async_remote_copy(
            src_ref=planes.at[block - hops], dst_ref=planes.at[block - hops],
            send_sem=rsend_sem.at[hops], recv_sem=rrecv_sem.at[hops],
            device_id={"tm": sibling}, device_id_type=MESH,
        )

    for hops in range(1, blocks):

        @pl.when((core == 1) & (block > hops))
        def _():
            pltpu.make_async_remote_copy(
                src_ref=planes.at[block - hops],
                dst_ref=planes.at[block - hops],
                send_sem=wsend_sem.at[hops],
                recv_sem=wrecv_sem.at[hops],
                device_id={"tm": me - hops * group},
                device_id_type=MESH,
            ).wait_recv()
            relay(hops).start()

    row = local[STEPS - 1 : STEPS]
    chunk_ends[0:1] = row
    for c in range(1, count):
        push = local[c * STEPS + STEPS - 1 : c * STEPS + STEPS]
        if c % 2:
            row = row_step(eye, ends[c], row, push)
            chunk_ends[c : c + 1] = to_row(eye, row)
        else:
            row = column_step(ends[c], row, push)
            chunk_ends[c : c + 1] = row

    carriers[block] = segments[0, place]
    for hops in range(1, blocks):

        @pl.when(block > hops)
        def _():
            @pl.when(core == 0)
            def _():
                relay(hops).wait_recv()

            carriers[block - hops] = product(planes[block - hops], carriers[block - hops + 1])

    for k in range(1, blocks):
        carriers[k] = jnp.where(k <= block, carriers[k].T, 0.0)

    @pl.loop(0, chips)
    def _(to):
        @pl.when(to != chip)
        def _():
            code(to).wait_send()
            weight(to).wait_send()

    for hops in range(1, blocks):

        @pl.when((core == 1) & (block > 0) & (block + hops < blocks))
        def _():
            forward(hops).wait_send()

        @pl.when((core == 1) & (block > hops))
        def _():
            relay(hops).wait_send()

    @pl.loop(home + group, n)
    def _(target):
        offset(target, carried, carries, me, crecv_sem.at[block]).wait_send()

    @pl.loop(me + 1, home + group)
    def _(target):
        offset(target, shift, shifts, place, srecv_sem.at[place]).wait_send()

    for plane in range(blocks - 1):

        @pl.when(block > plane)
        def _():
            four = carries.at[pl.ds(plane * group, group)]
            pltpu.make_async_remote_copy(
                src_ref=four, dst_ref=four, send_sem=ssend_sem.at[plane], recv_sem=crecv_sem.at[plane],
                device_id={"tm": sibling}, device_id_type=MESH,
            ).wait_recv()

    @pl.loop(home, me)
    def _(source):
        at = lax.rem(source, group)
        offset(source, shift, shifts, at, srecv_sem.at[at]).wait_recv()

    gathered = jnp.where(jnp.logical_and(eye, me == 0), start[...], 0.0)
    for q in range(group - 1):
        gathered += near[q] * shifts[q, 0:1]
    for k in range(1, blocks):
        sent = carries[(k - 1) * group, 0:1]
        for q in range(1, group):
            sent += carries[(k - 1) * group + q, 0:1]
        gathered += carriers[k] * sent
    entry = jnp.sum(gathered, axis=1, keepdims=True)
    inside = to_row(eye, entry)

    for c in range(count):
        if c:
            column = row_step(eye, heads[c - 1], inside, chunk_ends[c - 1 : c])
        else:
            column = entry
        for step in range(STEPS):
            t = c * STEPS + step
            out[t : t + 1] = column_step(prefix[t], column, local[t : t + 1])


VMEM = pl.BlockSpec(memory_space=pltpu.VMEM)
SMEM = pl.BlockSpec(memory_space=pltpu.SMEM)
HBM = pl.BlockSpec(memory_space=pltpu.HBM)
LIMIT = 62 * 1024 * 1024


def shards(n, frames, levels, initial_state, transitions, gain, pixel_mode, pixel_weight):
    group, chips = GROUP, n // 2
    blocks = n // group
    span = levels.shape[0]
    depth, states = transitions.shape[0], transitions.shape[1]
    pixels = frames.shape[0]
    count = span // STEPS
    square = (states, states)
    dma = pltpu.SemaphoreType.DMA
    return pl.pallas_call(
        functools.partial(fused_kernel, n),
        out_shape=pltpu.VMEM((span, states), F32),
        in_specs=[SMEM] + [HBM] * 6,
        out_specs=VMEM,
        scratch_shapes=[
            pltpu.VMEM((2, pixels, n * span), BF16),
            pltpu.VMEM((n * span, 2 * pixels), BF16),
            pltpu.VMEM((chips, span, states), F32),
            pltpu.VMEM((chips, span, states), jnp.int16),
            pltpu.VMEM((chips, span, states), jnp.int16),
            pltpu.VMEM((1, states), F32),
            pltpu.VMEM((chips, 1, states), F32),
            pltpu.VMEM((depth, *square), F32),
            pltpu.VMEM((depth, *square), F32),
            pltpu.VMEM((depth, 2 * states, 2 * states), BF16),
            pltpu.VMEM((span, *square), F32),
            pltpu.VMEM((count, *square), F32),
            pltpu.VMEM((count, *square), F32),
            pltpu.VMEM((count, *square), F32),
            pltpu.VMEM((count, *square), F32),
            pltpu.VMEM((group, *square), F32),
            pltpu.VMEM((2, group, *square), F32),
            pltpu.VMEM(square, F32),
            pltpu.VMEM((blocks, *square), F32),
            pltpu.VMEM((blocks, *square), F32),
            pltpu.VMEM((group, *square), F32),
            pltpu.VMEM(square, BF16),
            pltpu.VMEM((n, pixels), jnp.int32),
            pltpu.VMEM((n, pixels), BF16),
            pltpu.VMEM((n, pixels), F32),
            pltpu.VMEM((1, states), F32),
            pltpu.VMEM((2 * pixels, states), BF16),
            pltpu.VMEM((span, states), F32),
            pltpu.VMEM((count, states), F32),
            pltpu.VMEM((8, states), F32),
            pltpu.VMEM((group, 8, states), F32),
            pltpu.VMEM((8, states), F32),
            pltpu.VMEM((n, 8, states), F32),
            pltpu.SMEM((span,), jnp.int32),
            dma((6,)),
            dma,
            dma,
            dma((chips,)),
            dma((chips,)),
            dma((chips,)),
            dma((chips,)),
            dma,
            dma,
            dma((2,)),
            dma((2,)),
            dma((blocks,)),
            dma((blocks,)),
            dma((blocks,)),
            dma((blocks,)),
            dma((n,)),
            dma((group,)),
            dma((blocks,)),
            pltpu.SemaphoreType.REGULAR((chips,)),
            pltpu.SemaphoreType.REGULAR,
        ],
        compiler_params=pltpu.CompilerParams(
            collective_id=0, has_side_effects=True, vmem_limit_bytes=LIMIT
        ),
        name="filter",
    )(
        levels,
        frames,
        transitions,
        gain,
        pixel_mode.reshape(n, pixels),
        pixel_weight.reshape(n, pixels),
        initial_state.reshape(1, states),
    )


def solution(mesh):
    in_specs = (P("tm", "parts"), P(("parts", "tm")), P("parts"), P(), P(), P(), P())
    out_specs = P(("parts", "tm"), None)
    return jax.shard_map(
        functools.partial(shards, mesh.shape["tm"]),
        mesh=mesh,
        in_specs=in_specs,
        out_specs=out_specs,
        check_vma=False,
    )
```

```python
import functools

import jax
import jax.numpy as jnp
from jax import lax
from jax.experimental import pallas as pl
from jax.experimental.pallas import tpu as pltpu
from jax.sharding import PartitionSpec as P

MESH = pl.DeviceIdType.MESH
F32 = jnp.float32
BF16 = jnp.bfloat16
STEPS = 8
EARLY = 4
GROUP = 4
TOP = 32000.0


def halves(x):
    high = x.astype(BF16)
    return high, (x - high.astype(F32)).astype(BF16)


def left_pair(x):
    high, low = halves(x)
    return jnp.concatenate([high, low], axis=1)


def right_pair(y):
    pair = left_pair(y)
    return jnp.concatenate([pair, pair], axis=0)


def joined(pair):
    return pair[:, : pair.shape[1] // 2] + pair[:, pair.shape[1] // 2 :]


def product(x, y):
    return joined(jnp.dot(left_pair(x), right_pair(y), preferred_element_type=F32))


def diagonal(size):
    return lax.broadcasted_iota(jnp.int32, (size, size), 0) == lax.broadcasted_iota(
        jnp.int32, (size, size), 1
    )


def to_column(eye, row):
    return jnp.sum(jnp.where(eye, row, 0.0), axis=1, keepdims=True)


def to_row(eye, column):
    return jnp.sum(jnp.where(eye, column, 0.0), axis=0, keepdims=True)


def row_step(eye, matrix, row, push):
    return jnp.sum(matrix * row + jnp.where(eye, push, 0.0), axis=1, keepdims=True)


def column_step(flipped, column, push):
    return jnp.sum(flipped * column, axis=0, keepdims=True) + push


def fused_kernel(
    n,
    levels, frames_in, table_in, gain_in, modes_in, weights_in, start_in,
    out,
    raw, turned, sums, coded, arrived, scale, scales, table, flipped, pairs, prefix, foreign, heads, ends, tails, maps, segments, whole, planes, carriers, near,
    gain, modes, weights, heavy, start, projector, local, chunk_ends, shift, shifts, carried, carries, twin_levels,
    load_sem, swap_send, swap_recv, send_sem, recv_sem, ksend_sem, krecv_sem, lsend_sem, lrecv_sem, msend_sem, mrecv_sem, wsend_sem, wrecv_sem, rsend_sem, rrecv_sem, ssend_sem, srecv_sem, crecv_sem, ready, passed,
):
    group = GROUP
    me = lax.axis_index("tm")
    core, chip, chips = lax.rem(me, 2), me // 2, n // 2
    place = lax.rem(me, group)
    home = me - place
    sibling = me + 1 - 2 * core
    twin_place = lax.rem(place + 2, group)
    twin = home + twin_place
    block, blocks = me // group, n // group
    span = out.shape[0]
    states = gain.shape[0]
    pixels = raw.shape[1]
    count = span // STEPS
    loads = [
        pltpu.make_async_copy(source, target, load_sem.at[i])
        for i, (source, target) in enumerate(
            [
                (frames_in, raw.at[0]), (modes_in, modes), (weights_in, weights),
                (table_in, table), (gain_in, gain), (start_in, start),
            ]
        )
    ]
    for load in loads:
        load.start()

    barrier = pltpu.get_barrier_semaphore()

    def ahead(which):
        return jnp.maximum(which + lax.rem(which, 2) - 3, 0)

    far = ahead(chip)

    @pl.when(core == 0)
    def _():
        pl.semaphore_signal(barrier, inc=1, device_id={"tm": sibling}, device_id_type=MESH)

    @pl.loop(chip + 1, chips)
    def _(other):
        to = 2 * other + jnp.where(chip < ahead(other), 1, 0)
        pl.semaphore_signal(barrier, inc=1, device_id={"tm": to}, device_id_type=MESH)

    @pl.when(place >= 2)
    def _():
        pl.semaphore_signal(barrier, inc=1, device_id={"tm": home}, device_id_type=MESH)

    @pl.when(core == 1)
    def _():
        pl.semaphore_wait(barrier, 1 + 2 * far)
        pl.semaphore_signal(passed, inc=1, device_id={"tm": sibling}, device_id_type=MESH)

    @pl.when(core == 0)
    def _():
        pl.semaphore_wait(passed, 1)

    swap = pltpu.make_async_remote_copy(
        src_ref=frames_in, dst_ref=raw.at[1], send_sem=swap_send, recv_sem=swap_recv,
        device_id={"tm": sibling}, device_id_type=MESH,
    )
    swap.start()
    tell = pltpu.make_async_remote_copy(
        src_ref=levels, dst_ref=twin_levels, send_sem=lsend_sem, recv_sem=lrecv_sem,
        device_id={"tm": twin}, device_id_type=MESH,
    )

    def announce(low, high):
        @pl.loop(low, high)
        def _(other):
            pl.semaphore_signal(ready.at[chip], inc=1, device_id={"tm": 2 * other + core}, device_id_type=MESH)

    announce(0, far)

    def code(to):
        return pltpu.make_async_remote_copy(
            src_ref=coded.at[to], dst_ref=arrived.at[chip], send_sem=send_sem.at[to], recv_sem=recv_sem.at[chip],
            device_id={"tm": 2 * to + core}, device_id_type=MESH,
        )

    def weight(to):
        return pltpu.make_async_remote_copy(
            src_ref=scale, dst_ref=scales.at[chip], send_sem=ksend_sem.at[to], recv_sem=krecv_sem.at[chip],
            device_id={"tm": 2 * to + core}, device_id_type=MESH,
        )

    def arrival(source, slots, sent, received):
        return pltpu.make_async_remote_copy(
            src_ref=slots.at[source], dst_ref=slots.at[source], send_sem=sent.at[source], recv_sem=received.at[source],
            device_id={"tm": 2 * source + core}, device_id_type=MESH,
        )

    eye = diagonal(states)
    channels = lax.broadcasted_iota(jnp.int32, (states, pixels), 0)
    for load in loads[:3]:
        load.wait()
    heavy[...] = weights[...].astype(F32)
    for half, owner in enumerate((me, sibling)):
        projector[half * pixels : (half + 1) * pixels] = (
            jnp.where(
                modes[pl.ds(owner, 1)] == channels, heavy[pl.ds(owner, 1)], 0.0
            ).T.astype(BF16)
        )
    for at in range(0, n * span, 128):
        turned[at : at + 128, 0:pixels] = raw[0, :, at : at + 128].T

    @pl.when(core == 0)
    def _():
        pl.semaphore_wait(barrier, 2 * (chip - far) + jnp.where(place < 2, 2, 0))
        pl.semaphore_signal(passed, inc=1, device_id={"tm": sibling}, device_id_type=MESH)

    @pl.when(core == 1)
    def _():
        pl.semaphore_wait(passed, 1)

    announce(far, chip)

    tell.start()
    swap.wait()
    for at in range(0, n * span, 128):
        turned[at : at + 128, pixels : 2 * pixels] = raw[1, :, at : at + 128].T

    most = jnp.zeros((1, states), F32)
    for k in range(chips):
        sums[k] = jnp.dot(
            turned[pl.ds(pl.multiple_of((2 * k + core) * span, span), span)],
            projector[...],
            preferred_element_type=F32,
        )
        most = jnp.maximum(most, jnp.max(jnp.abs(sums[k]), axis=0, keepdims=True))
    most = jnp.maximum(most, 1e-30)
    scale[...] = most * (1.0 / TOP)
    finer = TOP / most
    for k in range(chips):
        coded[k] = jnp.round(sums[k] * finer).astype(jnp.int32).astype(jnp.int16)

    @pl.loop(0, chip)
    def _(to):
        weight(to).start()
        code(to).start()

    arrived[chip] = coded[chip]
    scales[chip] = scale[...]

    loads[3].wait()
    for level in range(table.shape[0]):
        other = table[level].T
        flipped[level] = other
        pairs[level] = right_pair(other)

    def prefix_step(step):
        for chunk in range(count):
            t = chunk * STEPS + step
            prefix[t] = joined(
                jnp.dot(left_pair(prefix[t - 1]), pairs[levels[t]], preferred_element_type=F32)
            )

    for chunk in range(count):
        prefix[chunk * STEPS] = flipped[levels[chunk * STEPS]]
    for step in range(1, EARLY):
        prefix_step(step)

    def meet(low, high):
        @pl.loop(jnp.minimum(low, chips), jnp.minimum(high, chips))
        def _(other):
            pl.semaphore_wait(ready.at[other], 1)
            weight(other).start()
            code(other).start()

    meet(chip + 1, 2 * block + 4)
    for step in range(EARLY, STEPS):
        prefix_step(step)

    spans = [prefix[chunk * STEPS + STEPS - 1] for chunk in range(count)]
    firsts = list(spans)
    for chunk in range(count):
        ends[chunk] = spans[chunk].T if chunk % 2 else spans[chunk]
    width = 1
    while width < count:
        for chunk in range(count):
            if chunk & width:
                base = (chunk // width) * width - 1
                spans[chunk] = product(spans[base], spans[chunk])
        width *= 2
    maps[place] = spans[count - 1]

    def shared(which):
        at = (place, twin_place)[which]
        return pltpu.make_async_remote_copy(
            src_ref=maps.at[at], dst_ref=maps.at[at], send_sem=msend_sem.at[which], recv_sem=mrecv_sem.at[which],
            device_id={"tm": sibling}, device_id_type=MESH,
        )

    shared(0).start()

    meet(2 * block + 4, chips)
    tell.wait()
    for chunk in range(count):
        foreign[chunk] = flipped[twin_levels[chunk * STEPS]]
    for step in range(1, STEPS):
        for chunk in range(count):
            foreign[chunk] = joined(
                jnp.dot(
                    left_pair(foreign[chunk]), pairs[twin_levels[chunk * STEPS + step]],
                    preferred_element_type=F32,
                )
            )
    others = [foreign[chunk] for chunk in range(count)]
    while len(others) > 1:
        others = [product(others[i], others[i + 1]) for i in range(0, len(others), 2)]
    maps[twin_place] = others[0]
    shared(1).start()

    tail = firsts[count - 1]
    for chunk in range(count - 2, -1, -1):
        tails[chunk] = tail.T
        if chunk:
            tail = product(firsts[chunk], tail)
    for chunk in range(count - 1):
        heads[chunk] = spans[chunk].T

    for load in loads[4:]:
        load.wait()
    turned_gain = gain[...].astype(F32).T.astype(BF16)
    unit = jnp.where(eye, 1.0, 0.0)
    none = jnp.zeros((states, states), F32)

    def shared_in(which):
        at = lax.rem(sibling, group) if which == 0 else lax.rem(sibling + 2, group)
        return pltpu.make_async_remote_copy(
            src_ref=maps.at[at], dst_ref=maps.at[at], send_sem=msend_sem.at[which], recv_sem=mrecv_sem.at[which],
            device_id={"tm": sibling}, device_id_type=MESH,
        )

    for which in range(2):
        shared_in(which).wait_recv()
        shared(which).wait_send()
    chains = {}
    for i in range(group):
        chains[i, i] = unit
        chains[i, i + 1] = maps[i]
    chains[0, 2] = product(chains[0, 1], chains[1, 2])
    chains[2, 4] = product(chains[2, 3], chains[3, 4])
    chains[0, 4] = product(chains[0, 2], chains[2, 4])
    whole[...] = chains[0, group]

    def forward(hops):
        return pltpu.make_async_remote_copy(
            src_ref=whole,
            dst_ref=planes.at[block],
            send_sem=wsend_sem.at[hops],
            recv_sem=wrecv_sem.at[hops],
            device_id={"tm": me + hops * group},
            device_id_type=MESH,
        )

    for hops in range(1, blocks):

        @pl.when((core == 1) & (block > 0) & (block + hops < blocks))
        def _():
            forward(hops).start()

    chains[1, 3] = product(chains[1, 2], chains[2, 3])
    chains[0, 3] = product(chains[0, 2], chains[2, 3])
    chains[1, 4] = product(chains[1, 2], chains[2, 4])
    for i in range(group):
        segments[0, i] = chains[0, i]
        segments[1, i] = chains[i + 1, group] if i + 1 < group else unit

    for p in range(1, group):

        @pl.when(place == p)
        def _():
            for q in range(p):
                near[q] = chains[q + 1, p].T

    @pl.loop(place, group)
    def _(q):
        near[q] = none
        shifts[q] = jnp.zeros((8, states), F32)

    @pl.loop(home, n)
    def _(source):
        carries[source] = jnp.zeros((8, states), F32)

    seed = jnp.where(me == 0, jnp.sum(maps[0].T * start[...], axis=1, keepdims=True), 0.0)

    measured = jnp.zeros((span, states), F32)
    for k in range(chips):

        @pl.when(chip != k)
        def _():
            arrival(k, arrived, send_sem, recv_sem).wait_recv()
            arrival(k, scales, ksend_sem, krecv_sem).wait_recv()

        measured += arrived[k].astype(jnp.int32).astype(F32) * scales[k, 0:1]
    local[...] = jnp.dot(measured.astype(BF16), turned_gain, preferred_element_type=F32)
    held = [to_column(eye, local[c * STEPS : c * STEPS + 1]) for c in range(count)]
    for step in range(1, STEPS):
        for c in range(count):
            t = c * STEPS + step
            push = local[t : t + 1]
            if step % 2:
                held[c] = column_step(flipped[levels[t]], held[c], push)
                local[t : t + 1] = held[c]
            else:
                held[c] = row_step(eye, table[levels[t]], held[c], push)
                local[t : t + 1] = to_row(eye, held[c])
    gathered = jnp.where(eye, local[span - 1 : span], 0.0)
    for c in range(count - 1):
        gathered += tails[c] * local[c * STEPS + STEPS - 1 : c * STEPS + STEPS]
    final = jnp.sum(gathered, axis=1, keepdims=True) + seed
    shift[...] = jnp.broadcast_to(to_row(eye, final), shift.shape)
    def offset(target, ref, slots, at, received):
        return pltpu.make_async_remote_copy(
            src_ref=ref,
            dst_ref=slots.at[at],
            send_sem=ssend_sem.at[target],
            recv_sem=received,
            device_id={"tm": target},
            device_id_type=MESH,
        )

    @pl.loop(me + 1, home + group)
    def _(target):
        offset(target, shift, shifts, place, srecv_sem.at[place]).start()

    carried[...] = jnp.broadcast_to(
        jnp.sum(segments[1, place] * final, axis=0, keepdims=True), carried.shape
    )

    @pl.loop(home + group, n)
    def _(target):
        offset(target, carried, carries, me, crecv_sem.at[block]).start()

    def relay(hops):
        return pltpu.make_async_remote_copy(
            src_ref=planes.at[block - hops], dst_ref=planes.at[block - hops],
            send_sem=rsend_sem.at[hops], recv_sem=rrecv_sem.at[hops],
            device_id={"tm": sibling}, device_id_type=MESH,
        )

    for hops in range(1, blocks):

        @pl.when((core == 1) & (block > hops))
        def _():
            pltpu.make_async_remote_copy(
                src_ref=planes.at[block - hops],
                dst_ref=planes.at[block - hops],
                send_sem=wsend_sem.at[hops],
                recv_sem=wrecv_sem.at[hops],
                device_id={"tm": me - hops * group},
                device_id_type=MESH,
            ).wait_recv()
            relay(hops).start()

    row = local[STEPS - 1 : STEPS]
    chunk_ends[0:1] = row
    for c in range(1, count):
        push = local[c * STEPS + STEPS - 1 : c * STEPS + STEPS]
        if c % 2:
            row = row_step(eye, ends[c], row, push)
            chunk_ends[c : c + 1] = to_row(eye, row)
        else:
            row = column_step(ends[c], row, push)
            chunk_ends[c : c + 1] = row

    carriers[block] = segments[0, place]
    for hops in range(1, blocks):

        @pl.when(block > hops)
        def _():
            @pl.when(core == 0)
            def _():
                relay(hops).wait_recv()

            carriers[block - hops] = product(planes[block - hops], carriers[block - hops + 1])

    for k in range(1, blocks):
        carriers[k] = jnp.where(k <= block, carriers[k].T, 0.0)

    @pl.loop(0, chips)
    def _(to):
        @pl.when(to != chip)
        def _():
            code(to).wait_send()
            weight(to).wait_send()

    for hops in range(1, blocks):

        @pl.when((core == 1) & (block > 0) & (block + hops < blocks))
        def _():
            forward(hops).wait_send()

        @pl.when((core == 1) & (block > hops))
        def _():
            relay(hops).wait_send()

    @pl.loop(home + group, n)
    def _(target):
        offset(target, carried, carries, me, crecv_sem.at[block]).wait_send()

    @pl.loop(me + 1, home + group)
    def _(target):
        offset(target, shift, shifts, place, srecv_sem.at[place]).wait_send()

    for plane in range(blocks - 1):

        @pl.when(block > plane)
        def _():
            four = carries.at[pl.ds(plane * group, group)]
            pltpu.make_async_remote_copy(
                src_ref=four, dst_ref=four, send_sem=ssend_sem.at[plane], recv_sem=crecv_sem.at[plane],
                device_id={"tm": sibling}, device_id_type=MESH,
            ).wait_recv()

    gathered = jnp.where(jnp.logical_and(eye, me == 0), start[...], 0.0)
    for k in range(1, blocks):
        sent = carries[(k - 1) * group, 0:1]
        for q in range(1, group):
            sent += carries[(k - 1) * group + q, 0:1]
        gathered += carriers[k] * sent

    @pl.loop(home, me)
    def _(source):
        at = lax.rem(source, group)
        offset(source, shift, shifts, at, srecv_sem.at[at]).wait_recv()

    for q in range(group - 1):
        gathered += near[q] * shifts[q, 0:1]
    entry = jnp.sum(gathered, axis=1, keepdims=True)
    inside = to_row(eye, entry)

    for c in range(count):
        if c:
            column = row_step(eye, heads[c - 1], inside, chunk_ends[c - 1 : c])
        else:
            column = entry
        for step in range(STEPS):
            t = c * STEPS + step
            out[t : t + 1] = column_step(prefix[t], column, local[t : t + 1])


VMEM = pl.BlockSpec(memory_space=pltpu.VMEM)
SMEM = pl.BlockSpec(memory_space=pltpu.SMEM)
HBM = pl.BlockSpec(memory_space=pltpu.HBM)
LIMIT = 62 * 1024 * 1024


def shards(n, frames, levels, initial_state, transitions, gain, pixel_mode, pixel_weight):
    group, chips = GROUP, n // 2
    blocks = n // group
    span = levels.shape[0]
    depth, states = transitions.shape[0], transitions.shape[1]
    pixels = frames.shape[0]
    count = span // STEPS
    square = (states, states)
    dma = pltpu.SemaphoreType.DMA
    return pl.pallas_call(
        functools.partial(fused_kernel, n),
        out_shape=pltpu.VMEM((span, states), F32),
        in_specs=[SMEM] + [HBM] * 6,
        out_specs=VMEM,
        scratch_shapes=[
            pltpu.VMEM((2, pixels, n * span), BF16),
            pltpu.VMEM((n * span, 2 * pixels), BF16),
            pltpu.VMEM((chips, span, states), F32),
            pltpu.VMEM((chips, span, states), jnp.int16),
            pltpu.VMEM((chips, span, states), jnp.int16),
            pltpu.VMEM((1, states), F32),
            pltpu.VMEM((chips, 1, states), F32),
            pltpu.VMEM((depth, *square), F32),
            pltpu.VMEM((depth, *square), F32),
            pltpu.VMEM((depth, 2 * states, 2 * states), BF16),
            pltpu.VMEM((span, *square), F32),
            pltpu.VMEM((count, *square), F32),
            pltpu.VMEM((count, *square), F32),
            pltpu.VMEM((count, *square), F32),
            pltpu.VMEM((count, *square), F32),
            pltpu.VMEM((group, *square), F32),
            pltpu.VMEM((2, group, *square), F32),
            pltpu.VMEM(square, F32),
            pltpu.VMEM((blocks, *square), F32),
            pltpu.VMEM((blocks, *square), F32),
            pltpu.VMEM((group, *square), F32),
            pltpu.VMEM(square, BF16),
            pltpu.VMEM((n, pixels), jnp.int32),
            pltpu.VMEM((n, pixels), BF16),
            pltpu.VMEM((n, pixels), F32),
            pltpu.VMEM((1, states), F32),
            pltpu.VMEM((2 * pixels, states), BF16),
            pltpu.VMEM((span, states), F32),
            pltpu.VMEM((count, states), F32),
            pltpu.VMEM((8, states), F32),
            pltpu.VMEM((group, 8, states), F32),
            pltpu.VMEM((8, states), F32),
            pltpu.VMEM((n, 8, states), F32),
            pltpu.SMEM((span,), jnp.int32),
            dma((6,)),
            dma,
            dma,
            dma((chips,)),
            dma((chips,)),
            dma((chips,)),
            dma((chips,)),
            dma,
            dma,
            dma((2,)),
            dma((2,)),
            dma((blocks,)),
            dma((blocks,)),
            dma((blocks,)),
            dma((blocks,)),
            dma((n,)),
            dma((group,)),
            dma((blocks,)),
            pltpu.SemaphoreType.REGULAR((chips,)),
            pltpu.SemaphoreType.REGULAR,
        ],
        compiler_params=pltpu.CompilerParams(
            collective_id=0, has_side_effects=True, vmem_limit_bytes=LIMIT
        ),
        name="filter",
    )(
        levels,
        frames,
        transitions,
        gain,
        pixel_mode.reshape(n, pixels),
        pixel_weight.reshape(n, pixels),
        initial_state.reshape(1, states),
    )


def solution(mesh):
    in_specs = (P("tm", "parts"), P(("parts", "tm")), P("parts"), P(), P(), P(), P())
    out_specs = P(("parts", "tm"), None)
    return jax.shard_map(
        functools.partial(shards, mesh.shape["tm"]),
        mesh=mesh,
        in_specs=in_specs,
        out_specs=out_specs,
        check_vma=False,
    )
```
